32 devices in a mesh: req: 16 (over z, x, core), tp: 2 (over y).
Axes of the slice: x: 2, y: 2, z: 4, core: 2. Of those that a mesh axis runs over, the one named last changes fastest.
Arguments:
- queries: bfloat16 [2048, 16, 192], P('req', 'tp'), may hold values from -160 to 160
- stretch_cache: bfloat16 [2048, 576], P('req'), may hold values from -6 to 6
- prefix_pool: bfloat16 [192, 64, 576], P('req'), may hold values from -6 to 6
- page_table: int32 [16, 12], P('req'), may hold values from 0 to 11, each once within a row
- prefix_len: int32 [16], replicated, may hold values from 1 to 768, 6144 in all
- prompt_cache: bfloat16 [2, 256, 576], P(None, 'req'), may hold values from -6 to 6
- prompt_len: int32 [2], replicated, may hold values from 1 to 256, 384 in all
- group_ids: int32 [16], replicated, may hold values from 0 to 1
- absorb_weight: bfloat16 [16, 128, 512], P('tp'), may hold values from -0.5 to 0.5
- value_weight: bfloat16 [16, 512, 128], P('tp'), may hold values from -1 to 1
- out_weight: bfloat16 [2048, 2048], P('tp'), may hold values from -0.125 to 0.125
- residual: bfloat16 [2048, 2048], P('req', 'tp'), may hold values from -20 to 20
- norm_gain: bfloat16 [2048], P('tp'), may hold values from 0.099609375 to 1.8984375
- routes: int32 [2048, 6], P('req'), may hold values from 0 to 15, all different within a row; in each aligned block of 128 rows (0 to 127, 128 to 255, ...) at most 64 rows name the same one
- route_weight: float32 [2048, 6], P('req'), may hold values from 0.05 to 0.45
- gate_weight: bfloat16 [16, 2048, 1408], P('req', None, 'tp'), may hold values from -0.125 to 0.125
- up_weight: bfloat16 [16, 2048, 1408], P('req', None, 'tp'), may hold values from -0.125 to 0.125
- down_weight: bfloat16 [16, 1408, 2048], P('req', 'tp'), may hold values from -0.15625 to 0.15625
Outputs:
- attended: bfloat16 [2048, 2048], P('req', 'tp')
- mixed: bfloat16 [2048, 2048], P('req', 'tp')
The draws below stay inside these ranges and needn't reach their ends.
Inputs may be any that keep to these rules, and one draw needn't show every extreme that they name: `page_table`: every row of a request is an order of its 12 pages. `prefix_len`: one request has a prefix of exactly 768. `routes`: in the rows of one request no expert is named more than 64 times, a bound that some block reaches.
All inputs are finite; a program needn't handle non-finite values.
Results may differ from the reference program's by a relative error of at most 0.023.
Values may be sent and summed in bfloat16 or wider, within the bound.
A program may use at most 64 MiB of HBM per device.

```python
import math
import jax
import jax.numpy as jnp
import numpy as np
from jax import lax

D = 2048
HEADS = 16
NOPE = 128
ROPE = 64
VDIM = 128
RANK = 512
FF_EXP = 1408
TOP = 6
TOK_DEV = 128
PAGE = 64
PAGES = 12
REQS = 16
TOKENS = 2048
EXPERTS = 16
LMAX = 768
SHARED = 256
CAP = 64
N_TP = 2


def attention_draw(key):
    base = jax.random.fold_in(key, 7)
    key_one, key_two = jax.random.split(base, 2)
    stretch = jnp.clip(jax.random.normal(key_one, (TOKENS, RANK + ROPE), jnp.float32), -6.0, 6.0)
    query = jnp.clip(jax.random.normal(key_two, (TOKENS, HEADS, NOPE + ROPE), jnp.float32), -6.0, 6.0)
    return (stretch, query)


def draw_queries(key, part):
    return attention_draw(key)[1].astype(jnp.bfloat16)


def draw_stretch_cache(key, part):
    return attention_draw(key)[0].astype(jnp.bfloat16)


def draw_residual(key, part):
    key_one, key_two, key_three = jax.random.split(jax.random.fold_in(key, 11), 3)
    column = jnp.arange(D).astype(jnp.float32) / D
    row_scale = 0.5 * jnp.exp(jax.random.uniform(key_two, (TOKENS, 1), jnp.float32, 0.0, math.log(10.0)))
    values = jnp.clip(jax.random.normal(key_one, (TOKENS, D), jnp.float32), -4.0, 4.0)
    rise = jnp.exp(math.log(30.0) * (column - 1.0))
    column_scale = jnp.exp(jax.random.uniform(key_three, (D,), jnp.float32, math.log(0.5), 0.0)) * rise
    return (values * row_scale * column_scale[None, :]).astype(jnp.bfloat16)


def set_ends(result, key, low, high):
    shape = result.shape
    spot = [jax.random.randint(jax.random.fold_in(key, axis), (), 0, shape[axis]) for axis in range(len(shape))]
    result = result.at[tuple(spot)].set(low)
    longest = shape.index(max(shape))
    spot[longest] = (spot[longest] + 1) % shape[longest]
    return result.at[tuple(spot)].set(high)


def shard_levels(own_key, dims, cuts, least, high):
    level, own = 1.0, jax.random.fold_in(own_key, 6)
    for axis_at, shards_of in cuts:
        steps = jnp.exp(jax.random.uniform(jax.random.fold_in(own, axis_at), (shards_of,), jnp.float32, least / len(cuts), high / len(cuts)))
        level = level * jnp.repeat(steps, dims[axis_at] // shards_of).reshape([-1 if axis == axis_at else 1 for axis in range(len(dims))])
    return level


def profile(amount, total, limit, lean):
    portions = [(1 << 20) // math.isqrt(standing ** lean) + 1 for standing in range(2, amount + 1)]
    spare, counts = total - limit - (amount - 1), [1] * (amount - 1)
    while spare > 0:
        movable = [i for i in range(amount - 1) if counts[i] < limit]
        mass, left = sum([portions[i] for i in movable]), spare
        for i in movable:
            addition = min(limit - counts[i], max(1, left * portions[i] // mass), spare)
            counts[i] = counts[i] + addition
            spare = spare - addition
    return np.array([limit] + counts)


def uneven_parts(key, amount, total, bound, lean):
    if amount == 2:
        one = jax.random.randint(key, (), max(1, total - bound), min(bound, total - 1) + 1)
        return jnp.stack([one, total - one])
    tallies = jnp.asarray(profile(amount, total, bound, lean), jnp.int32)
    couples = (amount - 1) // 2
    source_of, receiver = tallies[1:1 + 2 * couples:2], tallies[2:2 + 2 * couples:2]
    margin = jnp.minimum(source_of - 1, bound - receiver)
    shifted = jax.random.randint(jax.random.fold_in(key, 1), (couples,), 0, 1 << 20) % (margin + 1)
    tallies = tallies.at[1:1 + 2 * couples:2].set(source_of - shifted).at[2:2 + 2 * couples:2].set(receiver + shifted)
    return tallies[jax.random.permutation(jax.random.fold_in(key, 2), amount)]


def assign_block(rng, own, number, rows, number_of, top, limit, skew):
    sequence = jax.random.permutation(rng, number_of)
    heavy_load, usual = load_shares(number_of, rows * top, limit, skew, True), load_shares(number_of, rows * top, limit, skew, False)
    places = jnp.arange(number_of)

    def named(lengths, turn):
        used = int((lengths > 0).sum())
        fixed = max(1, used // 4)
        passed = fixed + (places - fixed + turn * (used - fixed)) % max(1, number_of - fixed)
        return jnp.zeros((number_of,), jnp.int32).at[sequence[jnp.where(places < fixed, places, passed)]].set(jnp.asarray(lengths, jnp.int32))

    lengths = jnp.where(number % 4 == 0, named(heavy_load, number // 4), named(usual, number - number // 4 - 1))
    mixed = jax.random.permutation(jax.random.fold_in(own, 3), number_of)
    donor, taker = mixed[0:number_of // 2 * 2:2], mixed[1:number_of // 2 * 2:2]
    slack = jnp.minimum(lengths[donor] - 1, limit - lengths[taker]) // 2
    slack = jnp.where((donor == sequence[0]) | (taker == sequence[0]) | (lengths[taker] == 0), 0, jnp.maximum(slack, 0))
    passed = jax.random.randint(jax.random.fold_in(own, 4), (number_of // 2,), 0, 1 << 20) % (slack + 1)
    lengths = lengths.at[donor].add(-passed).at[taker].add(passed)
    items = jnp.searchsorted(jnp.cumsum(lengths), jnp.arange(rows * top), side="right").astype(jnp.int32)
    listing = items.reshape(top, rows).T
    listing = listing[jax.random.permutation(jax.random.fold_in(own, 1), rows)]
    turn = jax.random.randint(jax.random.fold_in(own, 2), (rows, 1), 0, top)
    return jnp.take_along_axis(listing, (jnp.arange(top)[None, :] + turn) % top, axis=1)


def load_shares(count, total, most, slope, full):
    weights = [(1 << 20) // math.isqrt(grade ** slope) + 1 for grade in range(1, count + 1)]
    largest = most if full else min(most, max(-(-total // count), total * weights[0] // sum(weights)))
    least = 1 if total - largest >= count - 1 else 0
    holding, spare = [largest] + [least] * (count - 1), total - largest - least * (count - 1)
    while spare > 0:
        free = [i for i in range(1, count) if holding[i] < largest] or [i for i in range(1, count) if holding[i] < most]
        mass, budget = sum([weights[i] for i in free]), spare
        for i in free:
            addition = min(most - holding[i], max(1, budget * weights[i] // mass), spare)
            holding[i] = holding[i] + addition
            spare = spare - addition
    return np.array(holding)


def centred(stream_key, dims, scale, limit, shards=(), kind=jnp.bfloat16):
    factor_of = shard_levels(stream_key, dims, shards, -0.22, 0.18) if shards else 1.0
    entries = jax.random.normal(stream_key, dims, jnp.float32) * scale * factor_of
    return jnp.minimum(jnp.maximum(entries, -limit), limit).astype(kind)


def setup_inputs(seed: int = 0) -> dict:
    splits = jax.random.split(jax.random.key(seed), 19)
    queries = draw_queries(jax.random.fold_in(splits[18], 71), 0)
    stretch_cache = draw_stretch_cache(jax.random.fold_in(splits[18], 71), 0)
    prefix_pool = centred(splits[2], (REQS * PAGES, PAGE, RANK + ROPE), 1.0, 6.0, ((0, 16),))
    page_table = jax.vmap(lambda own: jax.random.permutation(own, PAGES))(jax.random.split(splits[3], REQS)).reshape((REQS, PAGES)).astype(jnp.int32)
    prefix_len = uneven_parts(splits[4], REQS, REQS * LMAX // 2, LMAX, 2).astype(jnp.int32)
    prompt_cache = centred(splits[5], (2, SHARED, RANK + ROPE), 1.0, 6.0, ((1, 16),))
    prompt_len = uneven_parts(splits[6], 2, SHARED + SHARED // 2, SHARED, 0).astype(jnp.int32)
    group_ids = set_ends(jax.random.randint(splits[7], (REQS,), 0, 2), jax.random.fold_in(splits[7], 1), 0, 1).astype(jnp.int32)
    absorb_weight = centred(splits[8], (HEADS, NOPE, RANK), NOPE ** -0.5, 0.5, ((0, 2),))
    value_weight = centred(splits[9], (HEADS, RANK, VDIM), (RANK // 16) ** -0.5, 1.0, ((0, 2),))
    out_weight = centred(splits[10], (HEADS * VDIM, D), (HEADS * VDIM) ** -0.5, 0.125, ((0, 2),))
    residual = draw_residual(jax.random.fold_in(splits[18], 71), 0)
    norm_gain = jnp.clip(1.0 + 0.18 * jax.random.normal(splits[12], (D,), jnp.float32), 0.099609375, 1.8984375).astype(jnp.bfloat16)
    routes_keys = jax.random.split(jax.random.fold_in(splits[13], 1), TOKENS // TOK_DEV)
    routes_turns = jax.random.permutation(jax.random.fold_in(splits[13], 3), TOKENS // TOK_DEV)
    routes = jax.vmap(lambda own, number: assign_block(jax.random.fold_in(splits[13], 2), own, number, TOK_DEV, EXPERTS, TOP, CAP, 2))(routes_keys, routes_turns).reshape((TOKENS, TOP))
    route_weight = jnp.clip(0.05 + 0.39999999 * jax.random.uniform(splits[14], (TOKENS, TOP), jnp.float32) ** shard_levels(splits[14], (TOKENS, TOP), ((0, 16),), -0.2, 0.2), 0.05, 0.45)
    gate_weight = centred(splits[15], (EXPERTS, D, FF_EXP), D ** -0.5, 0.125, ((0, 16), (2, 2)))
    up_weight = centred(splits[16], (EXPERTS, D, FF_EXP), D ** -0.5, 0.125, ((0, 16), (2, 2)))
    down_weight = centred(splits[17], (EXPERTS, FF_EXP, D), FF_EXP ** -0.5, 0.15625, ((0, 16), (1, 2)))
    return dict(queries=queries, stretch_cache=stretch_cache, prefix_pool=prefix_pool, page_table=page_table, prefix_len=prefix_len, prompt_cache=prompt_cache, prompt_len=prompt_len, group_ids=group_ids, absorb_weight=absorb_weight, value_weight=value_weight, out_weight=out_weight, residual=residual, norm_gain=norm_gain, routes=routes, route_weight=route_weight, gate_weight=gate_weight, up_weight=up_weight, down_weight=down_weight)


NEGATIVE = -1e+30

def rounded(value):
    return lax.optimization_barrier(value.astype(jnp.bfloat16)).astype(jnp.float32)

def reference(queries, stretch_cache, prefix_pool, page_table, prefix_len, prompt_cache, prompt_len, group_ids, absorb_weight, value_weight, out_weight, residual, norm_gain, routes, route_weight, gate_weight, up_weight, down_weight):
    scale = 1.0 / math.sqrt(NOPE + ROPE)
    pools = prefix_pool.reshape(REQS, PAGES, PAGE, RANK + ROPE)
    absorb32 = absorb_weight.astype(jnp.float32)
    value32 = value_weight.astype(jnp.float32)
    span = SHARED + LMAX + TOK_DEV
    place = jnp.arange(span, dtype=jnp.int32)
    position = jnp.arange(TOK_DEV, dtype=jnp.int32)

    def one_request(item):
        query, stretch, pool, table, length, group = item
        q32 = query.astype(jnp.float32)
        nope_part = jnp.einsum('thn,hnr->thr', q32[:, :, :NOPE], absorb32)
        absorbed = rounded(jnp.concatenate([nope_part, q32[:, :, NOPE:]], axis=2))
        prompt = prompt_cache[group]
        prefix = pool[table].reshape(LMAX, RANK + ROPE)
        keys = jnp.concatenate([prompt, prefix, stretch], axis=0).astype(jnp.float32)
        in_prompt = place < prompt_len[group]
        in_prefix = (place >= SHARED) & (place < SHARED + length)
        in_stretch = (place >= SHARED + LMAX)[None, :] & ((place - SHARED - LMAX)[None, :] <= position[:, None])
        valid = (in_prompt | in_prefix)[None, :] | in_stretch
        scores = jnp.einsum('thc,kc->thk', absorbed, keys) * scale
        masked = jnp.where(valid[:, None, :], scores, NEGATIVE)
        top = lax.optimization_barrier(jnp.max(masked, axis=2, keepdims=True))
        weights = jnp.where(valid[:, None, :], jnp.exp(masked - top), 0.0)
        total = lax.optimization_barrier(jnp.sum(weights, axis=2, keepdims=True))
        latent = jnp.einsum('thk,kr->thr', rounded(weights), keys[:, :RANK]) / total
        latent = rounded(latent)
        return jnp.einsum('thr,hrv->thv', latent, value32).astype(jnp.bfloat16)
    heads_out = lax.map(one_request, (queries.reshape(REQS, TOK_DEV, HEADS, NOPE + ROPE), stretch_cache.reshape(REQS, TOK_DEV, RANK + ROPE), pools, page_table, prefix_len, group_ids))
    projected = jnp.dot(heads_out.reshape(TOKENS, HEADS * VDIM), out_weight, preferred_element_type=jnp.float32)
    attended = (residual.astype(jnp.float32) + projected).astype(jnp.bfloat16)
    stream = attended.astype(jnp.float32)
    square_mean = lax.optimization_barrier(jnp.mean(stream * stream, axis=1, keepdims=True))
    normed = (stream * lax.rsqrt(square_mean + 1e-06) * norm_gain.astype(jnp.float32)).astype(jnp.bfloat16)
    flat = routes.reshape(REQS, TOK_DEV * TOP).astype(jnp.int32)
    onehot = (flat[:, :, None] == jnp.arange(EXPERTS, dtype=jnp.int32)[None, None, :]).astype(jnp.int32)
    slot = (lax.optimization_barrier(jnp.sum(jnp.cumsum(onehot, axis=1) * onehot, axis=2)) - 1).astype(jnp.int32)
    source = jnp.arange(REQS, dtype=jnp.int32)[:, None]
    dest = (flat * (REQS * CAP) + source * CAP + slot).astype(jnp.int32).reshape(-1)
    token_index = (source * TOK_DEV + jnp.arange(TOK_DEV * TOP, dtype=jnp.int32)[None, :] // TOP).astype(jnp.int32).reshape(-1)
    token_of = jnp.full((EXPERTS * REQS * CAP,), TOKENS, dtype=jnp.int32).at[dest].set(token_index)
    weight_of = jnp.zeros((EXPERTS * REQS * CAP,), jnp.float32).at[dest].set(route_weight.reshape(-1).astype(jnp.float32))
    padded = jnp.concatenate([normed, jnp.zeros((1, D), jnp.bfloat16)], axis=0)

    def expert_step(total, item):
        index, weights, gate_w, up_w, down_w = item
        rows = padded[index]
        gate = jnp.dot(rows, gate_w, preferred_element_type=jnp.float32)
        up = jnp.dot(rows, up_w, preferred_element_type=jnp.float32)
        hidden = (jax.nn.silu(gate) * up).astype(jnp.bfloat16)
        groups = hidden.astype(jnp.float32).reshape(REQS * CAP, N_TP, FF_EXP // N_TP)
        downs = down_w.astype(jnp.float32).reshape(N_TP, FF_EXP // N_TP, D)
        parts = jnp.einsum('rgf,gfd->grd', groups, downs).astype(jnp.bfloat16)
        contrib = lax.optimization_barrier(jnp.sum(parts.astype(jnp.float32), axis=0)) * weights[:, None]
        return (total.at[index].add(contrib), None)
    start = jnp.zeros((TOKENS + 1, D), jnp.float32)
    total, _ = lax.scan(expert_step, start, (token_of.reshape(EXPERTS, REQS * CAP), weight_of.reshape(EXPERTS, REQS * CAP), gate_weight, up_weight, down_weight))
    mixed = (stream + total[:TOKENS]).astype(jnp.bfloat16)
    return (attended, mixed)
```

```python
import jax
import jax.numpy as jnp
from jax import lax
from jax.sharding import PartitionSpec as P

BLOCK_PAGES = 4
GATHER_LIMIT = 4096


NEGATIVE = -1e30
EPSILON = 1e-06


def fold_keys(state, rows, keys, valid, rank, scale):
    maxima, totals, accum = state
    scores = (
        lax.dot_general(rows, keys, (((1,), (1,)), ((), ())), preferred_element_type=jnp.float32)
        * scale
    )
    masked = jnp.where(valid, scores, NEGATIVE)
    newtop = jnp.maximum(maxima, jnp.max(masked, axis=1))
    weights = jnp.where(valid, jnp.exp(masked - newtop[:, None]), 0.0)
    factor = jnp.exp(maxima - newtop)
    totals = totals * factor + jnp.sum(weights, axis=1)
    accum = accum * factor[:, None] + jnp.dot(
        weights.astype(jnp.bfloat16), keys[:, :rank], preferred_element_type=jnp.float32
    )
    return (newtop, totals, accum)


def merge_states(first, second):
    newtop = jnp.maximum(first[0], second[0])
    factor_one = jnp.exp(first[0] - newtop)
    factor_two = jnp.exp(second[0] - newtop)
    totals = first[1] * factor_one + second[1] * factor_two
    accum = first[2] * factor_one[:, None] + second[2] * factor_two[:, None]
    return (newtop, totals, accum)


def run_blocks(state, rows, keys_all, count_blocks, length, block, rank, scale):

    def step(index, carry):
        keys = lax.dynamic_slice_in_dim(keys_all, index * block, block, 0)
        valid = (index * block + jnp.arange(block, dtype=jnp.int32))[None, :] < length
        return fold_keys(carry, rows, keys, valid, rank, scale)

    return lax.fori_loop(0, count_blocks, step, state)


def on_device(
    queries,
    stretch_cache,
    prefix_pool,
    page_table,
    prefix_len,
    prompt_cache,
    prompt_len,
    group_ids,
    absorb_weight,
    value_weight,
    out_weight,
    residual,
    norm_gain,
    routes,
    route_weight,
    gate_weight,
    up_weight,
    down_weight,
):
    tokens, heads, width = queries.shape
    nope = absorb_weight.shape[1]
    rank = value_weight.shape[1]
    scale = width ** (-0.5)
    nope_part = jnp.einsum(
        "thn,hnr->thr", queries[:, :, :nope], absorb_weight, preferred_element_type=jnp.float32
    )
    absorbed = jnp.concatenate(
        [nope_part, queries[:, :, nope:].astype(jnp.float32)], axis=2
    ).astype(jnp.bfloat16)
    rows = absorbed.reshape(tokens * heads, width - nope + rank)
    count = rows.shape[0]
    empty = (
        jnp.full((count,), NEGATIVE, jnp.float32),
        jnp.zeros((count,), jnp.float32),
        jnp.zeros((count, rank), jnp.float32),
    )
    me_index = lax.axis_index("req")
    group = group_ids[me_index]
    prompt_length = prompt_len[group]
    own_length = prefix_len[me_index]
    causal = (
        jnp.arange(tokens, dtype=jnp.int32)[None, :]
        <= (jnp.arange(count, dtype=jnp.int32) // heads)[:, None]
    )
    stretch_state = fold_keys(empty, rows, stretch_cache, causal, rank, scale)
    keys = lax.dynamic_index_in_dim(
        lax.all_gather(prompt_cache, "req", axis=1, tiled=True), group, 0, keepdims=False
    )
    valid = jnp.arange(keys.shape[0], dtype=jnp.int32)[None, :] < prompt_length
    prompt_state = fold_keys(empty, rows, keys, valid, rank, scale)
    block = BLOCK_PAGES * prefix_pool.shape[1]
    prefix = jnp.take(prefix_pool, page_table[0], axis=0).reshape(-1, prefix_pool.shape[2])
    mine_blocks = (own_length + block - 1) // block
    prefix_state = run_blocks(empty, rows, prefix, mine_blocks, own_length, block, rank, scale)
    state = merge_states(merge_states(stretch_state, prompt_state), prefix_state)
    latent = (state[2] / state[1][:, None]).astype(jnp.bfloat16).reshape(tokens, heads, rank)
    heads_out = jnp.einsum(
        "thr,hrv->thv", latent, value_weight, preferred_element_type=jnp.float32
    ).astype(jnp.bfloat16)
    projected = jnp.dot(
        heads_out.reshape(tokens, -1), out_weight, preferred_element_type=jnp.float32
    )
    attention_part = lax.psum_scatter(
        projected.astype(jnp.bfloat16), "tp", scatter_dimension=1, tiled=True
    ).astype(jnp.float32)
    attended = (residual.astype(jnp.float32) + attention_part).astype(jnp.bfloat16)
    stream = attended.astype(jnp.float32)
    squares = lax.psum(jnp.sum(stream * stream, axis=1), "tp")
    model_width = out_weight.shape[1]
    normed = (
        stream * lax.rsqrt(squares / model_width + EPSILON)[:, None] * norm_gain.astype(jnp.float32)
    ).astype(jnp.bfloat16)
    experts = lax.axis_size("req")
    if tokens * experts > GATHER_LIMIT:
        return exchange_slots(
            stream, normed, attended, routes, route_weight, gate_weight, up_weight, down_weight
        )
    return gather_tokens(
        stream, normed, attended, routes, route_weight, gate_weight, up_weight, down_weight
    )


def exchange_slots(
    stream, normed, attended, routes, route_weight, gate_weight, up_weight, down_weight
):
    tokens = routes.shape[0]
    experts = lax.axis_size("req")
    top = routes.shape[1]
    capacity = max(2, tokens * top * 4 // (3 * experts))
    flat = routes.reshape(-1)
    onehot = (flat[:, None] == jnp.arange(experts, dtype=jnp.int32)[None, :]).astype(jnp.int32)
    slot = jnp.sum(jnp.cumsum(onehot, axis=0) * onehot, axis=1) - 1
    dest = (flat * capacity + slot).reshape(tokens, top)
    places = jnp.arange(experts * capacity, dtype=jnp.int32)
    chooser = jnp.any(dest[None, :, :] == places[:, None, None], axis=2).astype(jnp.bfloat16)
    whole = lax.all_gather(normed, "tp", axis=1, tiled=True)
    buffer = (
        jnp.dot(chooser, whole, preferred_element_type=jnp.float32)
        .astype(jnp.bfloat16)
        .reshape(experts, capacity, -1)
    )
    received = lax.all_to_all(buffer, "req", split_axis=0, concat_axis=0, tiled=True)
    gate = jnp.einsum("snd,df->snf", received, gate_weight[0], preferred_element_type=jnp.float32)
    up = jnp.einsum("snd,df->snf", received, up_weight[0], preferred_element_type=jnp.float32)
    hidden = (jax.nn.silu(gate) * up).astype(jnp.bfloat16)
    part_out = jnp.einsum(
        "snf,fd->snd", hidden, down_weight[0], preferred_element_type=jnp.float32
    ).astype(jnp.bfloat16)
    returned = lax.all_to_all(part_out, "req", split_axis=0, concat_axis=0, tiled=True)
    flat_out = returned.reshape(experts * capacity, -1)
    combined = jnp.zeros((tokens, flat_out.shape[1]), jnp.float32)
    for choice_index in range(top):
        picked = jnp.take(flat_out, dest[:, choice_index], axis=0).astype(jnp.float32)
        combined = combined + route_weight[:, choice_index : choice_index + 1] * picked
    expert_part = lax.psum_scatter(
        combined.astype(jnp.bfloat16), "tp", scatter_dimension=1, tiled=True
    ).astype(jnp.float32)
    mixed = (stream + expert_part).astype(jnp.bfloat16)
    return (attended, mixed)


def gather_tokens(
    stream, normed, attended, routes, route_weight, gate_weight, up_weight, down_weight
):
    tokens, top = routes.shape
    experts = lax.axis_size("req")
    capacity = max(2, tokens * top * 4 // (3 * experts))
    choice = routes[:, :, None] == jnp.arange(experts, dtype=jnp.int32)[None, None, :]
    share = jnp.sum(jnp.where(choice, route_weight[:, :, None], 0.0), axis=1)
    mine = lax.all_to_all(share.T, "req", split_axis=0, concat_axis=0, tiled=True)
    named = mine > 0.0
    before = jnp.arange(tokens)[:, None] <= jnp.arange(tokens)[None, :]
    slot = jnp.dot(
        named.astype(jnp.bfloat16), before.astype(jnp.bfloat16), preferred_element_type=jnp.float32
    ).astype(jnp.int32) - 1
    chooser = (
        (slot[:, None, :] == jnp.arange(capacity, dtype=jnp.int32)[None, :, None])
        & named[:, None, :]
    ).astype(jnp.bfloat16)
    half = lax.all_gather(normed, "req", axis=0, tiled=True)
    whole = lax.all_gather(half, "tp", axis=1, tiled=True).reshape(experts, tokens, -1)
    rows = jnp.einsum("est,etd->esd", chooser, whole, preferred_element_type=jnp.float32)
    rows = rows.astype(jnp.bfloat16).reshape(experts * capacity, -1)
    gate = jnp.dot(rows, gate_weight[0], preferred_element_type=jnp.float32)
    up = jnp.dot(rows, up_weight[0], preferred_element_type=jnp.float32)
    hidden = (jax.nn.silu(gate) * up).astype(jnp.bfloat16)
    part = jnp.dot(hidden, down_weight[0], preferred_element_type=jnp.float32)
    part = part.astype(jnp.bfloat16).reshape(experts, capacity, -1)
    spread = jnp.einsum("est,esd->etd", chooser, part, preferred_element_type=jnp.float32)
    spread = (spread * mine[:, :, None]).astype(jnp.bfloat16).reshape(experts * tokens, -1)
    summed = lax.psum_scatter(spread, "req", scatter_dimension=0, tiled=True)
    expert_part = lax.psum_scatter(summed, "tp", scatter_dimension=1, tiled=True)
    mixed = (stream + expert_part.astype(jnp.float32)).astype(jnp.bfloat16)
    return (attended, mixed)


def solution(mesh):
    in_specs = (
        P("req", "tp", None),
        P("req", None),
        P("req", None, None),
        P("req", None),
        P(),
        P(None, "req", None),
        P(),
        P(),
        P("tp", None, None),
        P("tp", None, None),
        P("tp", None),
        P("req", "tp"),
        P("tp"),
        P("req", None),
        P("req", None),
        P("req", None, "tp"),
        P("req", None, "tp"),
        P("req", "tp", None),
    )
    out_specs = (P("req", "tp"), P("req", "tp"))
    return jax.shard_map(
        on_device, mesh=mesh, in_specs=in_specs, out_specs=out_specs, check_vma=False
    )
```

```python
import jax
import jax.numpy as jnp
from jax import lax
from jax.experimental import pallas as pl
from jax.experimental.pallas import tpu as pltpu
from jax.sharding import PartitionSpec as P

BLOCK_PAGES = 4


NEGATIVE = -1e30
EPSILON = 1e-06


def fold_keys(state, rows, keys, valid, rank, scale):
    maxima, totals, accum = state
    scores = (
        lax.dot_general(rows, keys, (((1,), (1,)), ((), ())), preferred_element_type=jnp.float32)
        * scale
    )
    masked = jnp.where(valid, scores, NEGATIVE)
    newtop = jnp.maximum(maxima, jnp.max(masked, axis=1))
    weights = jnp.where(valid, jnp.exp(masked - newtop[:, None]), 0.0)
    factor = jnp.exp(maxima - newtop)
    totals = totals * factor + jnp.sum(weights, axis=1)
    accum = accum * factor[:, None] + jnp.dot(
        weights.astype(jnp.bfloat16), keys[:, :rank], preferred_element_type=jnp.float32
    )
    return (newtop, totals, accum)


def merge_states(first, second):
    newtop = jnp.maximum(first[0], second[0])
    factor_one = jnp.exp(first[0] - newtop)
    factor_two = jnp.exp(second[0] - newtop)
    totals = first[1] * factor_one + second[1] * factor_two
    accum = first[2] * factor_one[:, None] + second[2] * factor_two[:, None]
    return (newtop, totals, accum)


def run_blocks(state, rows, keys_all, count_blocks, length, block, rank, scale):

    def step(index, carry):
        keys = lax.dynamic_slice_in_dim(keys_all, index * block, block, 0)
        valid = (index * block + jnp.arange(block, dtype=jnp.int32))[None, :] < length
        return fold_keys(carry, rows, keys, valid, rank, scale)

    return lax.fori_loop(0, count_blocks, step, state)


def on_device(
    queries,
    stretch_cache,
    prefix_pool,
    page_table,
    prefix_len,
    prompt_cache,
    prompt_len,
    group_ids,
    absorb_weight,
    value_weight,
    out_weight,
    residual,
    norm_gain,
    routes,
    route_weight,
    gate_weight,
    up_weight,
    down_weight,
):
    tokens, heads, width = queries.shape
    nope = absorb_weight.shape[1]
    rank = value_weight.shape[1]
    scale = width ** (-0.5)
    nope_part = jnp.einsum(
        "thn,hnr->thr", queries[:, :, :nope], absorb_weight, preferred_element_type=jnp.float32
    )
    absorbed = jnp.concatenate(
        [nope_part, queries[:, :, nope:].astype(jnp.float32)], axis=2
    ).astype(jnp.bfloat16)
    rows = absorbed.reshape(tokens * heads, width - nope + rank)
    count = rows.shape[0]
    empty = (
        jnp.full((count,), NEGATIVE, jnp.float32),
        jnp.zeros((count,), jnp.float32),
        jnp.zeros((count, rank), jnp.float32),
    )
    me_index = lax.axis_index("req")
    group = group_ids[me_index]
    prompt_length = prompt_len[group]
    own_length = prefix_len[me_index]
    causal = (
        jnp.arange(tokens, dtype=jnp.int32)[None, :]
        <= (jnp.arange(count, dtype=jnp.int32) // heads)[:, None]
    )
    stretch_state = fold_keys(empty, rows, stretch_cache, causal, rank, scale)
    keys = lax.dynamic_index_in_dim(
        lax.all_gather(prompt_cache, "req", axis=1, tiled=True), group, 0, keepdims=False
    )
    valid = jnp.arange(keys.shape[0], dtype=jnp.int32)[None, :] < prompt_length
    prompt_state = fold_keys(empty, rows, keys, valid, rank, scale)
    block = BLOCK_PAGES * prefix_pool.shape[1]
    prefix = jnp.take(prefix_pool, page_table[0], axis=0).reshape(-1, prefix_pool.shape[2])
    mine_blocks = (own_length + block - 1) // block
    prefix_state = run_blocks(empty, rows, prefix, mine_blocks, own_length, block, rank, scale)
    state = merge_states(merge_states(stretch_state, prompt_state), prefix_state)
    latent = (state[2] / state[1][:, None]).astype(jnp.bfloat16).reshape(tokens, heads, rank)
    heads_out = jnp.einsum(
        "thr,hrv->thv", latent, value_weight, preferred_element_type=jnp.float32
    ).astype(jnp.bfloat16)
    projected = jnp.dot(
        heads_out.reshape(tokens, -1), out_weight, preferred_element_type=jnp.float32
    )
    attention_part = lax.psum_scatter(
        projected.astype(jnp.bfloat16), "tp", scatter_dimension=1, tiled=True
    ).astype(jnp.float32)
    attended = (residual.astype(jnp.float32) + attention_part).astype(jnp.bfloat16)
    stream = attended.astype(jnp.float32)
    squares = lax.psum(jnp.sum(stream * stream, axis=1), "tp")
    model_width = out_weight.shape[1]
    normed = (
        stream * lax.rsqrt(squares / model_width + EPSILON)[:, None] * norm_gain.astype(jnp.float32)
    ).astype(jnp.bfloat16)
    return exchange_slots(
        stream, normed, attended, routes, route_weight, gate_weight, up_weight, down_weight
    )


def exchange_slots(
    stream, normed, attended, routes, route_weight, gate_weight, up_weight, down_weight
):
    tokens = routes.shape[0]
    experts = lax.axis_size("req")
    top = routes.shape[1]
    capacity = max(2, tokens * top * 4 // (3 * experts))
    flat = routes.reshape(-1)
    onehot = (flat[:, None] == jnp.arange(experts, dtype=jnp.int32)[None, :]).astype(jnp.int32)
    slot = jnp.sum(jnp.cumsum(onehot, axis=0) * onehot, axis=1) - 1
    dest = (flat * capacity + slot).reshape(tokens, top)
    places = jnp.arange(experts * capacity, dtype=jnp.int32)
    chooser = jnp.any(dest[None, :, :] == places[:, None, None], axis=2).astype(jnp.bfloat16)
    whole = lax.all_gather(normed, "tp", axis=1, tiled=True)
    buffer = (
        jnp.dot(chooser, whole, preferred_element_type=jnp.float32)
        .astype(jnp.bfloat16)
        .reshape(experts, capacity, -1)
    )
    received = lax.all_to_all(buffer, "req", split_axis=0, concat_axis=0, tiled=True)
    gate = jnp.einsum("snd,df->snf", received, gate_weight[0], preferred_element_type=jnp.float32)
    up = jnp.einsum("snd,df->snf", received, up_weight[0], preferred_element_type=jnp.float32)
    hidden = (jax.nn.silu(gate) * up).astype(jnp.bfloat16)
    part_out = jnp.einsum(
        "snf,fd->snd", hidden, down_weight[0], preferred_element_type=jnp.float32
    ).astype(jnp.bfloat16)
    returned = lax.all_to_all(part_out, "req", split_axis=0, concat_axis=0, tiled=True)
    flat_out = returned.reshape(experts * capacity, -1)
    combined = jnp.zeros((tokens, flat_out.shape[1]), jnp.float32)
    for choice_index in range(top):
        picked = jnp.take(flat_out, dest[:, choice_index], axis=0).astype(jnp.float32)
        combined = combined + route_weight[:, choice_index : choice_index + 1] * picked
    expert_part = lax.psum_scatter(
        combined.astype(jnp.bfloat16), "tp", scatter_dimension=1, tiled=True
    ).astype(jnp.float32)
    mixed = (stream + expert_part).astype(jnp.bfloat16)
    return (attended, mixed)


MESH = pl.DeviceIdType.MESH


def coordinates():
    me = lax.axis_index("req")
    return me // 4, (me // 2) % 2, me % 2, lax.axis_index("tp")


def place(z, x, core, y):
    return {"req": (z * 2 + x) * 2 + core, "tp": y}


def prompt_kernel(block_ref, share_ref, keys_ref, mine_ref, send, recv, send_w, recv_w, local):
    me = lax.axis_index("req")
    y = lax.axis_index("tp")
    barrier = pltpu.get_barrier_semaphore()
    for step in range(1, 16):
        pl.semaphore_signal(
            barrier, inc=1, device_id={"req": (me + step) % 16, "tp": y}, device_id_type=MESH
        )
    pl.semaphore_wait(barrier, 15)
    rows = pl.ds(pl.multiple_of(me * 16, 16), 16)

    def copies(step):
        peer = (me + step) % 16
        block = pltpu.make_async_remote_copy(
            block_ref, keys_ref.at[:, rows, :], send.at[step], recv.at[step],
            device_id={"req": peer, "tp": y}, device_id_type=MESH,
        )
        share = pltpu.make_async_remote_copy(
            share_ref.at[peer], mine_ref.at[me], send_w.at[step], recv_w.at[step],
            device_id={"req": peer, "tp": y}, device_id_type=MESH,
        )
        return block, share

    for step in range(1, 16):
        block, share = copies(step)
        block.start()
        share.start()
    own = pltpu.make_async_copy(block_ref, keys_ref.at[:, rows, :], local.at[0])
    own_share = pltpu.make_async_copy(share_ref.at[me], mine_ref.at[me], local.at[1])
    own.start()
    own_share.start()
    own.wait()
    own_share.wait()
    for step in range(1, 16):
        block, share = copies(step)
        block.wait()
        share.wait()


def share_prompts(prompt_cache, share):
    groups, rows, width = prompt_cache.shape
    tokens = share.shape[2]
    return pl.pallas_call(
        prompt_kernel,
        out_shape=(
            jax.ShapeDtypeStruct((groups, rows * 16, width), prompt_cache.dtype),
            jax.ShapeDtypeStruct((16, 1, tokens), jnp.float32),
        ),
        in_specs=[pl.BlockSpec(memory_space=pltpu.VMEM)] * 2,
        out_specs=(pl.BlockSpec(memory_space=pltpu.VMEM),) * 2,
        scratch_shapes=[pltpu.SemaphoreType.DMA((16,))] * 4 + [pltpu.SemaphoreType.DMA((2,))],
        compiler_params=pltpu.CompilerParams(collective_id=0, has_side_effects=True),
    )(prompt_cache, share)


def greet():
    z, x, core, y = coordinates()
    barrier = pltpu.get_barrier_semaphore()
    for peer in (place(z, 1 - x, core, y), place(z, x, core, 1 - y), place(z, x, 1 - core, y)):
        pl.semaphore_signal(barrier, inc=1, device_id=peer, device_id_type=MESH)

    @pl.when(z < 3)
    def _():
        pl.semaphore_signal(barrier, inc=1, device_id=place(z + 1, x, core, y), device_id_type=MESH)

    @pl.when(z > 0)
    def _():
        pl.semaphore_signal(barrier, inc=1, device_id=place(z - 1, x, core, y), device_id_type=MESH)

    pl.semaphore_wait(barrier, 3 + (1 - z // 3) + (z + 2) // 3)


def spread_tokens(whole, send, recv):
    z, x, core, y = coordinates()
    half_rows, half_cols = whole.shape[1] // 2, whole.shape[2] // 2

    def piece(zp, xp, yp, half, cp):
        return whole.at[
            (zp * 2 + xp) * 2 + cp,
            pl.ds(half * half_rows, half_rows),
            pl.ds(pl.multiple_of(yp * half_cols, half_cols), half_cols),
        ]

    def hop(zp, xp, yp, half, cp, kind, peer):
        slot = zp * 8 + xp * 4 + yp * 2 + half
        part = piece(zp, xp, yp, half, cp)
        return pltpu.make_async_remote_copy(
            part, part, send.at[kind, slot], recv.at[cp, slot], device_id=peer, device_id_type=MESH
        )

    up, down = place(z + 1, x, core, y), place(z - 1, x, core, y)
    over_x, over_y, other = place(z, 1 - x, core, y), place(z, x, core, 1 - y), place(z, x, 1 - core, y)

    def column(zp, finish):
        for half in range(2):
            for go, kind, peer in (
                ((zp <= z) & (z < 3), 0, up), ((zp >= z) & (z > 0), 1, down)
            ):
                @pl.when(go)
                def _(kind=kind, peer=peer):
                    copy = hop(zp, x, y, half, core, kind, peer)
                    copy.wait_send() if finish else copy.start()
        for kind, peer, half in ((2, over_x, 0), (3, over_y, 1), (2, over_x, 1), (3, over_y, 0)):
            copy = hop(zp, x, y, half, core, kind, peer)
            copy.wait_send() if finish else copy.start()
        for half in range(2):
            copy = hop(zp, x, y, half, core, 4, other)
            copy.wait_send() if finish else copy.start()

    def beside(zp, finish):
        if not finish:
            for half in range(2):
                hop(zp, 1 - x, y, half, core, 2, over_x).wait_recv()
                hop(zp, x, 1 - y, half, core, 3, over_y).wait_recv()
        copies = [hop(zp, 1 - x, y, 0, core, 3, over_y), hop(zp, x, 1 - y, 1, core, 2, over_x)]
        for half in range(2):
            copies.append(hop(zp, 1 - x, y, half, core, 4, other))
            copies.append(hop(zp, x, 1 - y, half, core, 4, other))
        for copy in copies:
            copy.wait_send() if finish else copy.start()

    def diagonal(zp, finish):
        for half in range(2):
            copy = hop(zp, 1 - x, 1 - y, half, core, 4, other)
            if finish:
                copy.wait_send()
            else:
                hop(zp, 1 - x, 1 - y, half, core, 2, over_x).wait_recv()
                copy.start()

    def each(distance, work):
        if distance == 0:
            work(z)
            return

        @pl.when(z + distance < 4)
        def _():
            work(z + distance)

        @pl.when(z - distance >= 0)
        def _():
            work(z - distance)

    def arrive(zp):
        for half in range(2):
            hop(zp, x, y, half, core, 0, over_x).wait_recv()
        column(zp, False)

    column(z, False)
    for distance in range(1, 4):
        each(distance, arrive)
        each(distance - 1, lambda zp: beside(zp, False))
        if distance > 1:
            each(distance - 2, lambda zp: diagonal(zp, False))
    each(3, lambda zp: beside(zp, False))
    each(2, lambda zp: diagonal(zp, False))
    each(3, lambda zp: diagonal(zp, False))

    def close(zp, carry):
        for xp in range(2):
            for yp in range(2):
                for half in range(2):
                    hop(zp, xp, yp, half, 1 - core, 4, other).wait_recv()
        column(zp, True)
        beside(zp, True)
        diagonal(zp, True)
        return carry

    lax.fori_loop(0, 4, close, 0)


def return_sums(compute, acc, core_in, x_diag, y_diag, x_in, y_in, up_in, down_in, sems):
    z, x, core, y = coordinates()
    rows, half_cols = acc.shape[2], acc.shape[3] // 2
    half_rows = rows // 2
    up, down = place(z + 1, x, core, y), place(z - 1, x, core, y)
    over_x, over_y, other = place(z, 1 - x, core, y), place(z, x, core, 1 - y), place(z, x, 1 - core, y)
    mine = pl.ds(pl.multiple_of(y * half_cols, half_cols), half_cols)
    theirs = pl.ds(pl.multiple_of((1 - y) * half_cols, half_cols), half_cols)
    top, low = pl.ds(0, half_rows), pl.ds(half_rows, half_rows)

    def copy(source, target, kind, zp, peer):
        return pltpu.make_async_remote_copy(
            source, target, sems.at[0, kind, zp], sems.at[1, kind, zp],
            device_id=peer, device_id_type=MESH,
        )

    def block(zp, xp, cp):
        return acc.at[zp, xp * 2 + cp]

    def core_copy(zp, xp):
        return copy(block(zp, xp, 1 - core), core_in.at[zp, xp], xp, zp, other)

    def diag_copies(zp):
        far = block(zp, 1 - x, core)
        return (
            copy(far.at[top, theirs], y_diag.at[zp], 2, zp, over_y),
            copy(far.at[low, theirs], x_diag.at[zp], 3, zp, over_x),
        )

    def free_copies(zp):
        return (
            copy(block(zp, 1 - x, core).at[low, mine], x_in.at[zp, low], 4, zp, over_x),
            copy(block(zp, x, core).at[top, theirs], y_in.at[zp, top], 5, zp, over_y),
        )

    def last_copies(zp):
        return (
            copy(block(zp, 1 - x, core).at[top, mine], x_in.at[zp, top], 6, zp, over_x),
            copy(block(zp, x, core).at[low, theirs], y_in.at[zp, low], 7, zp, over_y),
        )

    def up_copy(zp):
        return copy(block(zp, x, core).at[:, mine], up_in.at[zp], 8, zp, up)

    def down_copy(zp):
        return copy(block(zp, x, core).at[:, mine], down_in.at[zp], 9, zp, down)

    def add(target, *terms):
        total = target[...].astype(jnp.float32)
        for term in terms:
            total = total + term[...].astype(jnp.float32)
        target[...] = total.astype(target.dtype)

    def cores(zp):
        for xp in range(2):
            core_copy(zp, xp).wait_recv()
            add(block(zp, xp, core), core_in.at[zp, xp])
        for item in diag_copies(zp) + free_copies(zp):
            item.start()

    def corners(zp):
        from_y, from_x = diag_copies(zp)
        over_x_copy, over_y_copy = last_copies(zp)
        from_y.wait_recv()
        add(block(zp, 1 - x, core).at[top, mine], y_diag.at[zp])
        over_x_copy.start()
        from_x.wait_recv()
        add(block(zp, x, core).at[low, theirs], x_diag.at[zp])
        over_y_copy.start()

    def columns(zp):
        for item in free_copies(zp) + last_copies(zp):
            item.wait_recv()
        own = block(zp, x, core).at[:, mine]
        add(own, x_in.at[zp], y_in.at[zp])

        @pl.when((z > 0) & (zp >= z))
        def _():
            up_copy(zp).wait_recv()
            add(own, up_in.at[zp])

        @pl.when((z < 3) & (zp <= z))
        def _():
            down_copy(zp).wait_recv()
            add(own, down_in.at[zp])

        @pl.when(zp > z)
        def _():
            up_copy(zp).start()

        @pl.when(zp < z)
        def _():
            down_copy(zp).start()

    def turn(step):
        return (3 - step // 2) * (1 - step % 2) + (step // 2) * (step % 2)

    def stage(step, carry):
        @pl.when(step < 4)
        def _():
            zp = turn(step)
            compute(zp)
            for xp in range(2):
                core_copy(zp, xp).start()

        @pl.when((step >= 1) & (step < 5))
        def _():
            cores(turn(step - 1))

        @pl.when((step >= 2) & (step < 6))
        def _():
            corners(turn(step - 2))

        @pl.when(step >= 3)
        def _():
            columns(turn(step - 3))

        return carry

    lax.fori_loop(0, 7, stage, 0)

    def close(zp, carry):
        for xp in range(2):
            core_copy(zp, xp).wait_send()
        for item in diag_copies(zp) + free_copies(zp) + last_copies(zp):
            item.wait_send()

        @pl.when(zp > z)
        def _():
            up_copy(zp).wait_send()

        @pl.when(zp < z)
        def _():
            down_copy(zp).wait_send()

        return carry

    lax.fori_loop(0, 4, close, 0)
    return block(z, x, core).at[:, mine]


def expert_kernel(
    projected, residual, gain, chooser, slot_weight, gate_hbm, up_hbm, down_hbm,
    attended, mixed,
    whole, outgoing, incoming, squares_out, squares_in, gate_w, up_w, down_w, rows, hidden,
    acc, core_in, x_diag, y_diag, x_in, y_in, up_in, down_in,
    pair_sems, load_sems, send, recv, sems,
):
    z, x, core, y = coordinates()
    half_cols = residual.shape[1]
    loads = [
        pltpu.make_async_copy(source, target, load_sems.at[index])
        for index, (source, target) in enumerate(
            ((gate_hbm, gate_w), (up_hbm, up_w), (down_hbm, down_w))
        )
    ]
    for load in loads:
        load.start()
    mine = pl.ds(pl.multiple_of(y * half_cols, half_cols), half_cols)
    theirs = pl.ds(pl.multiple_of((1 - y) * half_cols, half_cols), half_cols)
    over_y = place(z, x, core, 1 - y)
    outgoing[...] = projected[:, theirs].astype(jnp.bfloat16)
    greet()
    swap = pltpu.make_async_remote_copy(
        outgoing, incoming, pair_sems.at[0], pair_sems.at[1], device_id=over_y, device_id_type=MESH
    )
    swap.start()
    swap.wait()
    stream = residual[...].astype(jnp.float32) + projected[:, mine] + incoming[...].astype(jnp.float32)
    attended[...] = stream.astype(jnp.bfloat16)
    stream = attended[...].astype(jnp.float32)
    sums = jnp.sum(stream * stream, axis=1, keepdims=True)
    squares_out[...] = jnp.broadcast_to(sums, squares_out.shape)
    pair = pltpu.make_async_remote_copy(
        squares_out, squares_in, pair_sems.at[2], pair_sems.at[3],
        device_id=over_y, device_id_type=MESH,
    )
    pair.start()
    pair.wait()
    both = sums + squares_in[:, :1]
    scaled = stream * lax.rsqrt(both / (2 * half_cols) + EPSILON) * gain[...].astype(jnp.float32)
    whole[(z * 2 + x) * 2 + core, :, mine] = scaled.astype(jnp.bfloat16)
    spread_tokens(whole, send, recv)
    for load in loads:
        load.wait()
    capacity = chooser.shape[1]

    def compute(zp):
        for index in range(4):
            picked = jnp.dot(
                chooser[zp * 4 + index], whole[zp * 4 + index], preferred_element_type=jnp.float32
            )
            rows[pl.ds(index * capacity, capacity), :] = picked.astype(jnp.bfloat16)
        gate = jnp.dot(rows[...], gate_w[...], preferred_element_type=jnp.float32)
        up = jnp.dot(rows[...], up_w[...], preferred_element_type=jnp.float32)
        level = slot_weight[pl.ds(pl.multiple_of(zp * 4 * capacity, 4 * capacity), 4 * capacity), :]
        hidden[...] = (gate / (1.0 + jnp.exp(-gate)) * up * level).astype(jnp.bfloat16)
        part = jnp.dot(hidden[...], down_w[...], preferred_element_type=jnp.float32)
        part = part.astype(jnp.bfloat16)
        for index in range(4):
            acc[zp, index] = lax.dot_general(
                chooser[zp * 4 + index], part[index * capacity : (index + 1) * capacity],
                (((0,), (0,)), ((), ())), preferred_element_type=jnp.float32,
            ).astype(jnp.bfloat16)

    own = return_sums(compute, acc, core_in, x_diag, y_diag, x_in, y_in, up_in, down_in, sems)
    mixed[...] = (attended[...].astype(jnp.float32) + own[...].astype(jnp.float32)).astype(jnp.bfloat16)


def run_experts(projected, residual, gain, chooser, slot_weight, gate_w, up_w, down_w):
    tokens, width = projected.shape
    half = residual.shape[1]
    capacity = chooser.shape[1]
    units = gate_w.shape[1]
    bf16, f32 = jnp.bfloat16, jnp.float32
    dma = pltpu.SemaphoreType.DMA
    vmem = pl.BlockSpec(memory_space=pltpu.VMEM)
    anywhere = pl.BlockSpec(memory_space=pl.ANY)
    return pl.pallas_call(
        expert_kernel,
        out_shape=(jax.ShapeDtypeStruct((tokens, half), bf16),) * 2,
        in_specs=[vmem] * 5 + [anywhere] * 3,
        out_specs=(vmem, vmem),
        scratch_shapes=[
            pltpu.VMEM((16, tokens, width), bf16),
            pltpu.VMEM((tokens, half), bf16),
            pltpu.VMEM((tokens, half), bf16),
            pltpu.VMEM((tokens, 128), f32),
            pltpu.VMEM((tokens, 128), f32),
            pltpu.VMEM((width, units), bf16),
            pltpu.VMEM((width, units), bf16),
            pltpu.VMEM((units, width), bf16),
            pltpu.VMEM((4 * capacity, width), bf16),
            pltpu.VMEM((4 * capacity, units), bf16),
            pltpu.VMEM((4, 4, tokens, width), bf16),
            pltpu.VMEM((4, 2, tokens, width), bf16),
            pltpu.VMEM((4, tokens // 2, half), bf16),
            pltpu.VMEM((4, tokens // 2, half), bf16),
            pltpu.VMEM((4, tokens, half), bf16),
            pltpu.VMEM((4, tokens, half), bf16),
            pltpu.VMEM((4, tokens, half), bf16),
            pltpu.VMEM((4, tokens, half), bf16),
            dma((4,)),
            dma((3,)),
            dma((5, 32)),
            dma((2, 32)),
            dma((2, 10, 4)),
        ],
        compiler_params=pltpu.CompilerParams(
            collective_id=1, has_side_effects=True, vmem_limit_bytes=58 << 20
        ),
    )(projected, residual, gain, chooser, slot_weight, gate_w, up_w, down_w)


def on_block(
    queries, stretch_cache, prefix_pool, page_table, prefix_len, prompt_cache, prompt_len,
    group_ids, absorb_weight, value_weight, out_weight, residual, norm_gain, routes,
    route_weight, gate_weight, up_weight, down_weight,
):
    tokens, heads, width = queries.shape
    nope, rank = absorb_weight.shape[1], value_weight.shape[1]
    experts, top = lax.axis_size("req"), routes.shape[1]
    capacity = max(2, tokens * top * 4 // (3 * experts))
    me = lax.axis_index("req")
    choice = routes[:, :, None] == jnp.arange(experts, dtype=jnp.int32)[None, None, :]
    share = jnp.sum(jnp.where(choice, route_weight[:, :, None], 0.0), axis=1)
    prompts, mine = share_prompts(prompt_cache, share.T[:, None, :])
    mine = mine[:, 0, :]
    named = mine > 0.0
    before = jnp.arange(tokens)[:, None] <= jnp.arange(tokens)[None, :]
    slot = jnp.dot(
        named.astype(jnp.bfloat16), before.astype(jnp.bfloat16), preferred_element_type=jnp.float32
    ).astype(jnp.int32) - 1
    picks = (
        slot[:, None, :] == jnp.arange(capacity, dtype=jnp.int32)[None, :, None]
    ) & named[:, None, :]
    chooser = picks.astype(jnp.bfloat16)
    slot_weight = jnp.sum(jnp.where(picks, mine[:, None, :], 0.0), axis=2).reshape(-1, 1)

    group = group_ids[me]
    pages, page = prefix_pool.shape[:2]
    order = jnp.arange(pages, dtype=jnp.int32)
    logical = jnp.sum(
        jnp.where(page_table[0][None, :] == order[:, None], order[None, :], 0), axis=1
    )
    prefix_at = (logical[:, None] * page + jnp.arange(page, dtype=jnp.int32)[None, :]).reshape(-1)
    prompt = lax.dynamic_index_in_dim(prompts, group, 0, keepdims=False)
    keys = jnp.concatenate(
        [stretch_cache, prompt, prefix_pool.reshape(pages * page, -1)], axis=0
    )
    seen = jnp.concatenate(
        [jnp.arange(prompt.shape[0]) < prompt_len[group], prefix_at < prefix_len[me]]
    )
    token = jnp.arange(tokens)
    visible = jnp.concatenate(
        [
            token[None, :] <= token[:, None],
            jnp.broadcast_to(seen[None, :], (tokens, seen.shape[0])),
        ],
        axis=1,
    )
    turned = jnp.transpose(queries, (1, 0, 2))
    absorbed = jnp.concatenate(
        [
            jnp.einsum(
                "htn,hnr->htr", turned[:, :, :nope], absorb_weight,
                preferred_element_type=jnp.float32,
            ).astype(jnp.bfloat16),
            turned[:, :, nope:],
        ],
        axis=2,
    )
    scores = jnp.einsum("htc,kc->htk", absorbed, keys, preferred_element_type=jnp.float32)
    scores = jnp.where(visible[None], scores * width ** (-0.5), NEGATIVE)
    weights = jnp.exp(scores - jnp.max(scores, axis=2, keepdims=True))
    weights = jnp.where(visible[None], weights, 0.0)
    totals = jnp.sum(weights, axis=2, keepdims=True)
    latent = jnp.einsum(
        "htk,kr->htr", weights.astype(jnp.bfloat16), keys[:, :rank],
        preferred_element_type=jnp.float32,
    )
    latent = (latent / totals).astype(jnp.bfloat16)
    heads_out = jnp.einsum(
        "htr,hrv->thv", latent, value_weight, preferred_element_type=jnp.float32
    ).astype(jnp.bfloat16)
    projected = jnp.dot(
        heads_out.reshape(tokens, -1), out_weight, preferred_element_type=jnp.float32
    )
    return run_experts(
        projected, residual, norm_gain[None, :], chooser, slot_weight,
        gate_weight[0], up_weight[0], down_weight[0],
    )


def solution(mesh):
    in_specs = (
        P("req", "tp", None),
        P("req", None),
        P("req", None, None),
        P("req", None),
        P(),
        P(None, "req", None),
        P(),
        P(),
        P("tp", None, None),
        P("tp", None, None),
        P("tp", None),
        P("req", "tp"),
        P("tp"),
        P("req", None),
        P("req", None),
        P("req", None, "tp"),
        P("req", None, "tp"),
        P("req", "tp", None),
    )
    out_specs = (P("req", "tp"), P("req", "tp"))
    body = on_block if mesh.shape["req"] == 16 and mesh.shape["tp"] == 2 else on_device
    return jax.shard_map(
        body, mesh=mesh, in_specs=in_specs, out_specs=out_specs, check_vma=False
    )
```

```python
import jax
import jax.numpy as jnp
from jax import lax
from jax.experimental import pallas as pl
from jax.experimental.pallas import tpu as pltpu
from jax.sharding import PartitionSpec as P

BLOCK_PAGES = 4


NEGATIVE = -1e30
EPSILON = 1e-06


def fold_keys(state, rows, keys, valid, rank, scale):
    maxima, totals, accum = state
    scores = (
        lax.dot_general(rows, keys, (((1,), (1,)), ((), ())), preferred_element_type=jnp.float32)
        * scale
    )
    masked = jnp.where(valid, scores, NEGATIVE)
    newtop = jnp.maximum(maxima, jnp.max(masked, axis=1))
    weights = jnp.where(valid, jnp.exp(masked - newtop[:, None]), 0.0)
    factor = jnp.exp(maxima - newtop)
    totals = totals * factor + jnp.sum(weights, axis=1)
    accum = accum * factor[:, None] + jnp.dot(
        weights.astype(jnp.bfloat16), keys[:, :rank], preferred_element_type=jnp.float32
    )
    return (newtop, totals, accum)


def merge_states(first, second):
    newtop = jnp.maximum(first[0], second[0])
    factor_one = jnp.exp(first[0] - newtop)
    factor_two = jnp.exp(second[0] - newtop)
    totals = first[1] * factor_one + second[1] * factor_two
    accum = first[2] * factor_one[:, None] + second[2] * factor_two[:, None]
    return (newtop, totals, accum)


def run_blocks(state, rows, keys_all, count_blocks, length, block, rank, scale):

    def step(index, carry):
        keys = lax.dynamic_slice_in_dim(keys_all, index * block, block, 0)
        valid = (index * block + jnp.arange(block, dtype=jnp.int32))[None, :] < length
        return fold_keys(carry, rows, keys, valid, rank, scale)

    return lax.fori_loop(0, count_blocks, step, state)


def on_device(
    queries,
    stretch_cache,
    prefix_pool,
    page_table,
    prefix_len,
    prompt_cache,
    prompt_len,
    group_ids,
    absorb_weight,
    value_weight,
    out_weight,
    residual,
    norm_gain,
    routes,
    route_weight,
    gate_weight,
    up_weight,
    down_weight,
):
    tokens, heads, width = queries.shape
    nope = absorb_weight.shape[1]
    rank = value_weight.shape[1]
    scale = width ** (-0.5)
    nope_part = jnp.einsum(
        "thn,hnr->thr", queries[:, :, :nope], absorb_weight, preferred_element_type=jnp.float32
    )
    absorbed = jnp.concatenate(
        [nope_part, queries[:, :, nope:].astype(jnp.float32)], axis=2
    ).astype(jnp.bfloat16)
    rows = absorbed.reshape(tokens * heads, width - nope + rank)
    count = rows.shape[0]
    empty = (
        jnp.full((count,), NEGATIVE, jnp.float32),
        jnp.zeros((count,), jnp.float32),
        jnp.zeros((count, rank), jnp.float32),
    )
    me_index = lax.axis_index("req")
    group = group_ids[me_index]
    prompt_length = prompt_len[group]
    own_length = prefix_len[me_index]
    causal = (
        jnp.arange(tokens, dtype=jnp.int32)[None, :]
        <= (jnp.arange(count, dtype=jnp.int32) // heads)[:, None]
    )
    stretch_state = fold_keys(empty, rows, stretch_cache, causal, rank, scale)
    keys = lax.dynamic_index_in_dim(
        lax.all_gather(prompt_cache, "req", axis=1, tiled=True), group, 0, keepdims=False
    )
    valid = jnp.arange(keys.shape[0], dtype=jnp.int32)[None, :] < prompt_length
    prompt_state = fold_keys(empty, rows, keys, valid, rank, scale)
    block = BLOCK_PAGES * prefix_pool.shape[1]
    prefix = jnp.take(prefix_pool, page_table[0], axis=0).reshape(-1, prefix_pool.shape[2])
    mine_blocks = (own_length + block - 1) // block
    prefix_state = run_blocks(empty, rows, prefix, mine_blocks, own_length, block, rank, scale)
    state = merge_states(merge_states(stretch_state, prompt_state), prefix_state)
    latent = (state[2] / state[1][:, None]).astype(jnp.bfloat16).reshape(tokens, heads, rank)
    heads_out = jnp.einsum(
        "thr,hrv->thv", latent, value_weight, preferred_element_type=jnp.float32
    ).astype(jnp.bfloat16)
    projected = jnp.dot(
        heads_out.reshape(tokens, -1), out_weight, preferred_element_type=jnp.float32
    )
    attention_part = lax.psum_scatter(
        projected.astype(jnp.bfloat16), "tp", scatter_dimension=1, tiled=True
    ).astype(jnp.float32)
    attended = (residual.astype(jnp.float32) + attention_part).astype(jnp.bfloat16)
    stream = attended.astype(jnp.float32)
    squares = lax.psum(jnp.sum(stream * stream, axis=1), "tp")
    model_width = out_weight.shape[1]
    normed = (
        stream * lax.rsqrt(squares / model_width + EPSILON)[:, None] * norm_gain.astype(jnp.float32)
    ).astype(jnp.bfloat16)
    return exchange_slots(
        stream, normed, attended, routes, route_weight, gate_weight, up_weight, down_weight
    )


def exchange_slots(
    stream, normed, attended, routes, route_weight, gate_weight, up_weight, down_weight
):
    tokens = routes.shape[0]
    experts = lax.axis_size("req")
    top = routes.shape[1]
    capacity = max(2, tokens * top * 4 // (3 * experts))
    flat = routes.reshape(-1)
    onehot = (flat[:, None] == jnp.arange(experts, dtype=jnp.int32)[None, :]).astype(jnp.int32)
    slot = jnp.sum(jnp.cumsum(onehot, axis=0) * onehot, axis=1) - 1
    dest = (flat * capacity + slot).reshape(tokens, top)
    places = jnp.arange(experts * capacity, dtype=jnp.int32)
    chooser = jnp.any(dest[None, :, :] == places[:, None, None], axis=2).astype(jnp.bfloat16)
    whole = lax.all_gather(normed, "tp", axis=1, tiled=True)
    buffer = (
        jnp.dot(chooser, whole, preferred_element_type=jnp.float32)
        .astype(jnp.bfloat16)
        .reshape(experts, capacity, -1)
    )
    received = lax.all_to_all(buffer, "req", split_axis=0, concat_axis=0, tiled=True)
    gate = jnp.einsum("snd,df->snf", received, gate_weight[0], preferred_element_type=jnp.float32)
    up = jnp.einsum("snd,df->snf", received, up_weight[0], preferred_element_type=jnp.float32)
    hidden = (jax.nn.silu(gate) * up).astype(jnp.bfloat16)
    part_out = jnp.einsum(
        "snf,fd->snd", hidden, down_weight[0], preferred_element_type=jnp.float32
    ).astype(jnp.bfloat16)
    returned = lax.all_to_all(part_out, "req", split_axis=0, concat_axis=0, tiled=True)
    flat_out = returned.reshape(experts * capacity, -1)
    combined = jnp.zeros((tokens, flat_out.shape[1]), jnp.float32)
    for choice_index in range(top):
        picked = jnp.take(flat_out, dest[:, choice_index], axis=0).astype(jnp.float32)
        combined = combined + route_weight[:, choice_index : choice_index + 1] * picked
    expert_part = lax.psum_scatter(
        combined.astype(jnp.bfloat16), "tp", scatter_dimension=1, tiled=True
    ).astype(jnp.float32)
    mixed = (stream + expert_part).astype(jnp.bfloat16)
    return (attended, mixed)


MESH = pl.DeviceIdType.MESH


def coordinates():
    me = lax.axis_index("req")
    return me // 4, (me // 2) % 2, me % 2, lax.axis_index("tp")


def place(z, x, core, y):
    return {"req": (z * 2 + x) * 2 + core, "tp": y}


def prompt_kernel(block_ref, share_ref, keys_ref, mine_ref, send, recv, send_w, recv_w, local):
    me = lax.axis_index("req")
    y = lax.axis_index("tp")
    barrier = pltpu.get_barrier_semaphore()
    for step in range(1, 16):
        pl.semaphore_signal(
            barrier, inc=1, device_id={"req": (me + step) % 16, "tp": y}, device_id_type=MESH
        )
    pl.semaphore_wait(barrier, 15)
    rows = pl.ds(pl.multiple_of(me * 16, 16), 16)

    def shares(step):
        peer = (me + step) % 16
        return pltpu.make_async_remote_copy(
            share_ref.at[peer], mine_ref.at[me], send_w.at[step], recv_w.at[step],
            device_id={"req": peer, "tp": y}, device_id_type=MESH,
        )

    core, other = me % 2, me + 1 - 2 * (me % 2)

    def relay(step):
        source = (me + 2 * step) % 16
        lines = pl.ds(pl.multiple_of(source * 16, 16), 16)
        arrival = pltpu.make_async_remote_copy(
            keys_ref.at[:, lines, :], keys_ref.at[:, lines, :], send.at[8 - step],
            recv.at[8 - step], device_id={"req": source, "tp": y}, device_id_type=MESH,
        )
        passing = pltpu.make_async_remote_copy(
            keys_ref.at[:, lines, :], keys_ref.at[:, lines, :], send.at[8 + source // 2],
            recv.at[8 + source // 2], device_id={"req": other, "tp": y}, device_id_type=MESH,
        )
        return arrival, passing

    def arriving(step):
        source = (me + 2 * step) % 16 + 1 - 2 * core
        lines = pl.ds(pl.multiple_of(source * 16, 16), 16)
        return pltpu.make_async_remote_copy(
            keys_ref.at[:, lines, :], keys_ref.at[:, lines, :], send.at[8 + source // 2],
            recv.at[8 + source // 2], device_id={"req": other, "tp": y}, device_id_type=MESH,
        )

    def direct(step):
        return pltpu.make_async_remote_copy(
            block_ref, keys_ref.at[:, rows, :], send.at[step], recv.at[step],
            device_id={"req": (me + 2 * step) % 16, "tp": y}, device_id_type=MESH,
        )

    home = pltpu.make_async_remote_copy(
        block_ref, keys_ref.at[:, rows, :], send.at[8 + me // 2], recv.at[8 + me // 2],
        device_id={"req": other, "tp": y}, device_id_type=MESH,
    )
    for step in range(1, 8):
        direct(step).start()
    home.start()
    for step in range(1, 16):
        shares(step).start()
    own = pltpu.make_async_copy(block_ref, keys_ref.at[:, rows, :], local.at[0])
    own_share = pltpu.make_async_copy(share_ref.at[me], mine_ref.at[me], local.at[1])
    own.start()
    own_share.start()
    own.wait()
    own_share.wait()
    for step in range(1, 8):
        arrival, passing = relay(step)
        arrival.wait_recv()
        passing.start()
    for step in range(8):
        arriving(step).wait_recv()
    home.wait_send()
    for step in range(1, 8):
        direct(step).wait_send()
        relay(step)[1].wait_send()
    for step in range(1, 16):
        shares(step).wait()


def share_prompts(prompt_cache, share):
    groups, rows, width = prompt_cache.shape
    tokens = share.shape[2]
    return pl.pallas_call(
        prompt_kernel,
        out_shape=(
            jax.ShapeDtypeStruct((groups, rows * 16, width), prompt_cache.dtype),
            jax.ShapeDtypeStruct((16, 1, tokens), jnp.float32),
        ),
        in_specs=[pl.BlockSpec(memory_space=pltpu.VMEM)] * 2,
        out_specs=(pl.BlockSpec(memory_space=pltpu.VMEM),) * 2,
        scratch_shapes=[pltpu.SemaphoreType.DMA((16,))] * 4 + [pltpu.SemaphoreType.DMA((2,))],
        compiler_params=pltpu.CompilerParams(collective_id=0, has_side_effects=True),
    )(prompt_cache, share)


def greet():
    z, x, core, y = coordinates()
    barrier = pltpu.get_barrier_semaphore()
    for peer in (place(z, 1 - x, core, y), place(z, x, core, 1 - y), place(z, x, 1 - core, y)):
        pl.semaphore_signal(barrier, inc=1, device_id=peer, device_id_type=MESH)

    @pl.when(z < 3)
    def _():
        pl.semaphore_signal(barrier, inc=1, device_id=place(z + 1, x, core, y), device_id_type=MESH)

    @pl.when(z > 0)
    def _():
        pl.semaphore_signal(barrier, inc=1, device_id=place(z - 1, x, core, y), device_id_type=MESH)

    pl.semaphore_wait(barrier, 3 + (1 - z // 3) + (z + 2) // 3)


def spread_tokens(whole, send, recv, finish):
    z, x, core, y = coordinates()
    half_rows, half_cols = whole.shape[1] // 2, whole.shape[2] // 2

    def piece(zp, xp, yp, half, cp):
        return whole.at[
            (zp * 2 + xp) * 2 + cp,
            pl.ds(half * half_rows, half_rows),
            pl.ds(pl.multiple_of(yp * half_cols, half_cols), half_cols),
        ]

    def hop(zp, xp, yp, half, cp, kind, peer):
        slot = zp * 8 + xp * 4 + yp * 2 + half
        part = piece(zp, xp, yp, half, cp)
        return pltpu.make_async_remote_copy(
            part, part, send.at[kind, slot], recv.at[cp, slot], device_id=peer, device_id_type=MESH
        )

    up, down = place(z + 1, x, core, y), place(z - 1, x, core, y)
    over_x, over_y, other = place(z, 1 - x, core, y), place(z, x, core, 1 - y), place(z, x, 1 - core, y)

    def column(zp, finish):
        for half in range(2):
            for go, kind, peer in (
                ((zp <= z) & (z < 3), 0, up), ((zp >= z) & (z > 0), 1, down)
            ):
                @pl.when(go)
                def _(kind=kind, peer=peer):
                    copy = hop(zp, x, y, half, core, kind, peer)
                    copy.wait_send() if finish else copy.start()
        for kind, peer, half in ((2, over_x, 0), (3, over_y, 1), (2, over_x, 1), (3, over_y, 0)):
            copy = hop(zp, x, y, half, core, kind, peer)
            copy.wait_send() if finish else copy.start()
        for half in range(2):
            copy = hop(zp, x, y, half, core, 4, other)
            copy.wait_send() if finish else copy.start()

    def beside(zp, finish):
        if not finish:
            for half in range(2):
                hop(zp, 1 - x, y, half, core, 2, over_x).wait_recv()
                hop(zp, x, 1 - y, half, core, 3, over_y).wait_recv()
        copies = [hop(zp, 1 - x, y, 0, core, 3, over_y), hop(zp, x, 1 - y, 1, core, 2, over_x)]
        for half in range(2):
            copies.append(hop(zp, 1 - x, y, half, core, 4, other))
            copies.append(hop(zp, x, 1 - y, half, core, 4, other))
        for copy in copies:
            copy.wait_send() if finish else copy.start()

    def diagonal(zp, finish):
        for half in range(2):
            copy = hop(zp, 1 - x, 1 - y, half, core, 4, other)
            if finish:
                copy.wait_send()
            else:
                hop(zp, 1 - x, 1 - y, half, core, 2, over_x).wait_recv()
                copy.start()

    def arrive(zp):
        for half in range(2):
            hop(zp, x, y, half, core, 0, over_x).wait_recv()
        column(zp, False)

    def ready(zp):
        for xp in range(2):
            for yp in range(2):
                for half in range(2):
                    hop(zp, xp, yp, half, 1 - core, 4, other).wait_recv()
        finish(zp)

    column(z, False)

    def turn(step, carry):
        for lag, work, first in (
            (0, arrive, 1), (2, lambda zp: beside(zp, False), 0),
            (4, lambda zp: diagonal(zp, False), 0), (5, ready, 0),
        ):
            item = step - lag
            distance = (item + 1) // 2
            zp = z + distance * (2 * (item % 2) - 1)

            @pl.when((item >= first) & (item < 7) & (zp >= 0) & (zp < 4))
            def _(work=work, zp=zp):
                work(zp)

        return carry

    lax.fori_loop(1, 12, turn, 0)

    def close(zp, carry):
        column(zp, True)
        beside(zp, True)
        diagonal(zp, True)
        return carry

    lax.fori_loop(0, 4, close, 0)


def core_hop(acc, core_in, sems, zp, xp):
    z, x, core, y = coordinates()
    return pltpu.make_async_remote_copy(
        acc.at[zp, xp * 2 + 1 - core], core_in.at[zp, xp], sems.at[0, xp, zp], sems.at[1, xp, zp],
        device_id=place(z, x, 1 - core, y), device_id_type=MESH,
    )


def return_sums(acc, core_in, x_diag, y_diag, x_in, y_in, up_in, down_in, sems):
    z, x, core, y = coordinates()
    rows, half_cols = acc.shape[2], acc.shape[3] // 2
    half_rows = rows // 2
    up, down = place(z + 1, x, core, y), place(z - 1, x, core, y)
    over_x, over_y, other = place(z, 1 - x, core, y), place(z, x, core, 1 - y), place(z, x, 1 - core, y)
    mine = pl.ds(pl.multiple_of(y * half_cols, half_cols), half_cols)
    theirs = pl.ds(pl.multiple_of((1 - y) * half_cols, half_cols), half_cols)
    top, low = pl.ds(0, half_rows), pl.ds(half_rows, half_rows)

    def copy(source, target, kind, zp, peer):
        return pltpu.make_async_remote_copy(
            source, target, sems.at[0, kind, zp], sems.at[1, kind, zp],
            device_id=peer, device_id_type=MESH,
        )

    def block(zp, xp, cp):
        return acc.at[zp, xp * 2 + cp]

    def core_copy(zp, xp):
        return core_hop(acc, core_in, sems, zp, xp)

    def diag_copies(zp):
        far = block(zp, 1 - x, core)
        return (
            copy(far.at[top, theirs], y_diag.at[zp], 2, zp, over_y),
            copy(far.at[low, theirs], x_diag.at[zp], 3, zp, over_x),
        )

    def free_copies(zp):
        return (
            copy(block(zp, 1 - x, core).at[low, mine], x_in.at[zp, low], 4, zp, over_x),
            copy(block(zp, x, core).at[top, theirs], y_in.at[zp, top], 5, zp, over_y),
        )

    def last_copies(zp):
        return (
            copy(block(zp, 1 - x, core).at[top, mine], x_in.at[zp, top], 6, zp, over_x),
            copy(block(zp, x, core).at[low, theirs], y_in.at[zp, low], 7, zp, over_y),
        )

    def up_copy(zp):
        return copy(block(zp, x, core).at[:, mine], up_in.at[zp], 8, zp, up)

    def down_copy(zp):
        return copy(block(zp, x, core).at[:, mine], down_in.at[zp], 9, zp, down)

    def add(target, *terms):
        total = target[...].astype(jnp.float32)
        for term in terms:
            total = total + term[...].astype(jnp.float32)
        target[...] = total.astype(target.dtype)

    def cores(zp):
        for xp in range(2):
            core_copy(zp, xp).wait_recv()
            add(block(zp, xp, core), core_in.at[zp, xp])
        for item in diag_copies(zp) + free_copies(zp):
            item.start()

    def corners(zp):
        from_y, from_x = diag_copies(zp)
        over_x_copy, over_y_copy = last_copies(zp)
        from_y.wait_recv()
        add(block(zp, 1 - x, core).at[top, mine], y_diag.at[zp])
        over_x_copy.start()
        from_x.wait_recv()
        add(block(zp, x, core).at[low, theirs], x_diag.at[zp])
        over_y_copy.start()

    def columns(zp):
        for item in free_copies(zp) + last_copies(zp):
            item.wait_recv()
        own = block(zp, x, core).at[:, mine]
        add(own, x_in.at[zp], y_in.at[zp])

        @pl.when((z > 0) & (zp >= z))
        def _():
            up_copy(zp).wait_recv()
            add(own, up_in.at[zp])

        @pl.when((z < 3) & (zp <= z))
        def _():
            down_copy(zp).wait_recv()
            add(own, down_in.at[zp])

        @pl.when(zp > z)
        def _():
            up_copy(zp).start()

        @pl.when(zp < z)
        def _():
            down_copy(zp).start()

    def turn(step):
        return (3 - step // 2) * (1 - step % 2) + (step // 2) * (step % 2)

    def stage(step, carry):
        @pl.when(step < 4)
        def _():
            cores(turn(step))

        @pl.when((step >= 1) & (step < 5))
        def _():
            corners(turn(step - 1))

        @pl.when(step >= 2)
        def _():
            columns(turn(step - 2))

        return carry

    lax.fori_loop(0, 6, stage, 0)

    def close(zp, carry):
        for xp in range(2):
            core_copy(zp, xp).wait_send()
        for item in diag_copies(zp) + free_copies(zp) + last_copies(zp):
            item.wait_send()

        @pl.when(zp > z)
        def _():
            up_copy(zp).wait_send()

        @pl.when(zp < z)
        def _():
            down_copy(zp).wait_send()

        return carry

    lax.fori_loop(0, 4, close, 0)
    return block(z, x, core).at[:, mine]


def expert_kernel(
    projected, residual, gain, chooser, slot_weight, gate_hbm, up_hbm, down_hbm,
    attended, mixed,
    whole, outgoing, incoming, squares_out, squares_in, gate_w, up_w, down_w, rows, hidden,
    acc, core_in, x_diag, y_diag, x_in, y_in, up_in, down_in,
    pair_sems, load_sems, send, recv, sems,
):
    z, x, core, y = coordinates()
    half_cols = residual.shape[1]
    loads = [
        pltpu.make_async_copy(source, target, load_sems.at[index])
        for index, (source, target) in enumerate(
            ((gate_hbm, gate_w), (up_hbm, up_w), (down_hbm, down_w))
        )
    ]
    for load in loads:
        load.start()
    mine = pl.ds(pl.multiple_of(y * half_cols, half_cols), half_cols)
    theirs = pl.ds(pl.multiple_of((1 - y) * half_cols, half_cols), half_cols)
    over_y = place(z, x, core, 1 - y)
    outgoing[...] = projected[:, theirs].astype(jnp.bfloat16)
    greet()
    swap = pltpu.make_async_remote_copy(
        outgoing, incoming, pair_sems.at[0], pair_sems.at[1], device_id=over_y, device_id_type=MESH
    )
    swap.start()
    swap.wait()
    stream = residual[...].astype(jnp.float32) + projected[:, mine] + incoming[...].astype(jnp.float32)
    attended[...] = stream.astype(jnp.bfloat16)
    stream = attended[...].astype(jnp.float32)
    sums = jnp.sum(stream * stream, axis=1, keepdims=True)
    squares_out[...] = jnp.broadcast_to(sums, squares_out.shape)
    pair = pltpu.make_async_remote_copy(
        squares_out, squares_in, pair_sems.at[2], pair_sems.at[3],
        device_id=over_y, device_id_type=MESH,
    )
    pair.start()
    pair.wait()
    both = sums + squares_in[:, :1]
    scaled = stream * lax.rsqrt(both / (2 * half_cols) + EPSILON) * gain[...].astype(jnp.float32)
    whole[(z * 2 + x) * 2 + core, :, mine] = scaled.astype(jnp.bfloat16)
    for load in loads:
        load.wait()
    capacity = chooser.shape[1]

    def compute(zp):
        for index in range(4):
            picked = jnp.dot(
                chooser[zp * 4 + index], whole[zp * 4 + index], preferred_element_type=jnp.float32
            )
            rows[pl.ds(index * capacity, capacity), :] = picked.astype(jnp.bfloat16)
        across = (((1,), (1,)), ((), ()))
        gate = lax.dot_general(rows[...], gate_w[...], across, preferred_element_type=jnp.float32)
        up = lax.dot_general(rows[...], up_w[...], across, preferred_element_type=jnp.float32)
        level = slot_weight[pl.ds(pl.multiple_of(zp * 4 * capacity, 4 * capacity), 4 * capacity), :]
        hidden[...] = (gate / (1.0 + jnp.exp(-gate)) * up * level).astype(jnp.bfloat16)
        part = jnp.dot(hidden[...], down_w[...], preferred_element_type=jnp.float32)
        part = part.astype(jnp.bfloat16)
        for index in range(4):
            acc[zp, index] = lax.dot_general(
                chooser[zp * 4 + index], part[index * capacity : (index + 1) * capacity],
                (((0,), (0,)), ((), ())), preferred_element_type=jnp.float32,
            ).astype(jnp.bfloat16)

        for xp in range(2):
            core_hop(acc, core_in, sems, zp, xp).start()

    spread_tokens(whole, send, recv, compute)
    own = return_sums(acc, core_in, x_diag, y_diag, x_in, y_in, up_in, down_in, sems)
    mixed[...] = (attended[...].astype(jnp.float32) + own[...].astype(jnp.float32)).astype(jnp.bfloat16)


def run_experts(projected, residual, gain, chooser, slot_weight, gate_w, up_w, down_w):
    tokens, width = projected.shape
    half = residual.shape[1]
    capacity = chooser.shape[1]
    units = gate_w.shape[0]
    bf16, f32 = jnp.bfloat16, jnp.float32
    dma = pltpu.SemaphoreType.DMA
    vmem = pl.BlockSpec(memory_space=pltpu.VMEM)
    anywhere = pl.BlockSpec(memory_space=pl.ANY)
    return pl.pallas_call(
        expert_kernel,
        out_shape=(jax.ShapeDtypeStruct((tokens, half), bf16),) * 2,
        in_specs=[vmem] * 5 + [anywhere] * 3,
        out_specs=(vmem, vmem),
        scratch_shapes=[
            pltpu.VMEM((16, tokens, width), bf16),
            pltpu.VMEM((tokens, half), bf16),
            pltpu.VMEM((tokens, half), bf16),
            pltpu.VMEM((tokens, 128), f32),
            pltpu.VMEM((tokens, 128), f32),
            pltpu.VMEM((units, width), bf16),
            pltpu.VMEM((units, width), bf16),
            pltpu.VMEM((units, width), bf16),
            pltpu.VMEM((4 * capacity, width), bf16),
            pltpu.VMEM((4 * capacity, units), bf16),
            pltpu.VMEM((4, 4, tokens, width), bf16),
            pltpu.VMEM((4, 2, tokens, width), bf16),
            pltpu.VMEM((4, tokens // 2, half), bf16),
            pltpu.VMEM((4, tokens // 2, half), bf16),
            pltpu.VMEM((4, tokens, half), bf16),
            pltpu.VMEM((4, tokens, half), bf16),
            pltpu.VMEM((4, tokens, half), bf16),
            pltpu.VMEM((4, tokens, half), bf16),
            dma((4,)),
            dma((3,)),
            dma((5, 32)),
            dma((2, 32)),
            dma((2, 10, 4)),
        ],
        compiler_params=pltpu.CompilerParams(
            collective_id=1, has_side_effects=True, vmem_limit_bytes=58 << 20
        ),
    )(projected, residual, gain, chooser, slot_weight, gate_w, up_w, down_w)


def on_block(
    queries, stretch_cache, prefix_pool, page_table, prefix_len, prompt_cache, prompt_len,
    group_ids, absorb_weight, value_weight, out_weight, residual, norm_gain, routes,
    route_weight, gate_weight, up_weight, down_weight,
):
    tokens, heads, width = queries.shape
    nope, rank = absorb_weight.shape[1], value_weight.shape[1]
    experts, top = lax.axis_size("req"), routes.shape[1]
    capacity = max(2, tokens * top * 4 // (3 * experts))
    me = lax.axis_index("req")
    choice = routes[:, :, None] == jnp.arange(experts, dtype=jnp.int32)[None, None, :]
    share = jnp.sum(jnp.where(choice, route_weight[:, :, None], 0.0), axis=1)
    prompts, mine = share_prompts(prompt_cache, share.T[:, None, :])
    mine = mine[:, 0, :]
    named = mine > 0.0
    before = jnp.arange(tokens)[:, None] <= jnp.arange(tokens)[None, :]
    slot = jnp.dot(
        named.astype(jnp.bfloat16), before.astype(jnp.bfloat16), preferred_element_type=jnp.float32
    ).astype(jnp.int32) - 1
    picks = (
        slot[:, None, :] == jnp.arange(capacity, dtype=jnp.int32)[None, :, None]
    ) & named[:, None, :]
    chooser = picks.astype(jnp.bfloat16)
    slot_weight = jnp.sum(jnp.where(picks, mine[:, None, :], 0.0), axis=2).reshape(-1, 1)

    requests = jnp.arange(group_ids.shape[0], dtype=jnp.int32) == me
    group = jnp.sum(jnp.where(requests, group_ids, 0))
    own_length = jnp.sum(jnp.where(requests, prefix_len, 0))
    prompt_length = jnp.where(group == 0, prompt_len[0], prompt_len[1])
    pages, page = prefix_pool.shape[:2]
    order = jnp.arange(pages, dtype=jnp.int32)
    logical = jnp.sum(
        jnp.where(page_table[0][None, :] == order[:, None], order[None, :], 0), axis=1
    )
    prefix_at = (logical[:, None] * page + jnp.arange(page, dtype=jnp.int32)[None, :]).reshape(-1)
    prompt = jnp.where(group == 0, prompts[0], prompts[1])
    keys = jnp.concatenate(
        [stretch_cache, prompt, prefix_pool.reshape(pages * page, -1)], axis=0
    )
    seen = jnp.concatenate(
        [jnp.arange(prompt.shape[0]) < prompt_length, prefix_at < own_length]
    )
    token = jnp.arange(tokens)
    visible = jnp.concatenate(
        [
            token[None, :] <= token[:, None],
            jnp.broadcast_to(seen[None, :], (tokens, seen.shape[0])),
        ],
        axis=1,
    )
    turned = jnp.transpose(queries, (1, 0, 2))
    absorbed = jnp.concatenate(
        [
            jnp.einsum(
                "htn,hnr->htr", turned[:, :, :nope], absorb_weight,
                preferred_element_type=jnp.float32,
            ).astype(jnp.bfloat16),
            turned[:, :, nope:],
        ],
        axis=2,
    )
    scores = jnp.einsum("htc,kc->htk", absorbed, keys, preferred_element_type=jnp.float32)
    scores = jnp.where(visible[None], scores * width ** (-0.5), NEGATIVE)
    weights = jnp.exp(scores - jnp.max(scores, axis=2, keepdims=True))
    weights = jnp.where(visible[None], weights, 0.0)
    totals = jnp.sum(weights, axis=2, keepdims=True)
    latent = jnp.einsum(
        "htk,kr->htr", weights.astype(jnp.bfloat16), keys[:, :rank],
        preferred_element_type=jnp.float32,
    )
    latent = (latent / totals).astype(jnp.bfloat16)
    heads_out = jnp.einsum(
        "htr,hrv->thv", latent, value_weight, preferred_element_type=jnp.float32
    ).astype(jnp.bfloat16)
    projected = jnp.dot(
        heads_out.reshape(tokens, -1), out_weight, preferred_element_type=jnp.float32
    )
    return run_experts(
        projected, residual, norm_gain[None, :], chooser, slot_weight,
        jnp.swapaxes(gate_weight[0], 0, 1), jnp.swapaxes(up_weight[0], 0, 1), down_weight[0],
    )


def solution(mesh):
    in_specs = (
        P("req", "tp", None),
        P("req", None),
        P("req", None, None),
        P("req", None),
        P(),
        P(None, "req", None),
        P(),
        P(),
        P("tp", None, None),
        P("tp", None, None),
        P("tp", None),
        P("req", "tp"),
        P("tp"),
        P("req", None),
        P("req", None),
        P("req", None, "tp"),
        P("req", None, "tp"),
        P("req", "tp", None),
    )
    out_specs = (P("req", "tp"), P("req", "tp"))
    body = on_block if mesh.shape["req"] == 16 and mesh.shape["tp"] == 2 else on_device
    return jax.shard_map(
        body, mesh=mesh, in_specs=in_specs, out_specs=out_specs, check_vma=False
    )
```

```python
import jax
import jax.numpy as jnp
from jax import lax
from jax.experimental import pallas as pl
from jax.experimental.pallas import tpu as pltpu
from jax.sharding import PartitionSpec as P

BLOCK_PAGES = 4


NEGATIVE = -1e30
EPSILON = 1e-06


def fold_keys(state, rows, keys, valid, rank, scale):
    maxima, totals, accum = state
    scores = (
        lax.dot_general(rows, keys, (((1,), (1,)), ((), ())), preferred_element_type=jnp.float32)
        * scale
    )
    masked = jnp.where(valid, scores, NEGATIVE)
    newtop = jnp.maximum(maxima, jnp.max(masked, axis=1))
    weights = jnp.where(valid, jnp.exp(masked - newtop[:, None]), 0.0)
    factor = jnp.exp(maxima - newtop)
    totals = totals * factor + jnp.sum(weights, axis=1)
    accum = accum * factor[:, None] + jnp.dot(
        weights.astype(jnp.bfloat16), keys[:, :rank], preferred_element_type=jnp.float32
    )
    return (newtop, totals, accum)


def merge_states(first, second):
    newtop = jnp.maximum(first[0], second[0])
    factor_one = jnp.exp(first[0] - newtop)
    factor_two = jnp.exp(second[0] - newtop)
    totals = first[1] * factor_one + second[1] * factor_two
    accum = first[2] * factor_one[:, None] + second[2] * factor_two[:, None]
    return (newtop, totals, accum)


def run_blocks(state, rows, keys_all, count_blocks, length, block, rank, scale):

    def step(index, carry):
        keys = lax.dynamic_slice_in_dim(keys_all, index * block, block, 0)
        valid = (index * block + jnp.arange(block, dtype=jnp.int32))[None, :] < length
        return fold_keys(carry, rows, keys, valid, rank, scale)

    return lax.fori_loop(0, count_blocks, step, state)


def on_device(
    queries,
    stretch_cache,
    prefix_pool,
    page_table,
    prefix_len,
    prompt_cache,
    prompt_len,
    group_ids,
    absorb_weight,
    value_weight,
    out_weight,
    residual,
    norm_gain,
    routes,
    route_weight,
    gate_weight,
    up_weight,
    down_weight,
):
    tokens, heads, width = queries.shape
    nope = absorb_weight.shape[1]
    rank = value_weight.shape[1]
    scale = width ** (-0.5)
    nope_part = jnp.einsum(
        "thn,hnr->thr", queries[:, :, :nope], absorb_weight, preferred_element_type=jnp.float32
    )
    absorbed = jnp.concatenate(
        [nope_part, queries[:, :, nope:].astype(jnp.float32)], axis=2
    ).astype(jnp.bfloat16)
    rows = absorbed.reshape(tokens * heads, width - nope + rank)
    count = rows.shape[0]
    empty = (
        jnp.full((count,), NEGATIVE, jnp.float32),
        jnp.zeros((count,), jnp.float32),
        jnp.zeros((count, rank), jnp.float32),
    )
    me_index = lax.axis_index("req")
    group = group_ids[me_index]
    prompt_length = prompt_len[group]
    own_length = prefix_len[me_index]
    causal = (
        jnp.arange(tokens, dtype=jnp.int32)[None, :]
        <= (jnp.arange(count, dtype=jnp.int32) // heads)[:, None]
    )
    stretch_state = fold_keys(empty, rows, stretch_cache, causal, rank, scale)
    keys = lax.dynamic_index_in_dim(
        lax.all_gather(prompt_cache, "req", axis=1, tiled=True), group, 0, keepdims=False
    )
    valid = jnp.arange(keys.shape[0], dtype=jnp.int32)[None, :] < prompt_length
    prompt_state = fold_keys(empty, rows, keys, valid, rank, scale)
    block = BLOCK_PAGES * prefix_pool.shape[1]
    prefix = jnp.take(prefix_pool, page_table[0], axis=0).reshape(-1, prefix_pool.shape[2])
    mine_blocks = (own_length + block - 1) // block
    prefix_state = run_blocks(empty, rows, prefix, mine_blocks, own_length, block, rank, scale)
    state = merge_states(merge_states(stretch_state, prompt_state), prefix_state)
    latent = (state[2] / state[1][:, None]).astype(jnp.bfloat16).reshape(tokens, heads, rank)
    heads_out = jnp.einsum(
        "thr,hrv->thv", latent, value_weight, preferred_element_type=jnp.float32
    ).astype(jnp.bfloat16)
    projected = jnp.dot(
        heads_out.reshape(tokens, -1), out_weight, preferred_element_type=jnp.float32
    )
    attention_part = lax.psum_scatter(
        projected.astype(jnp.bfloat16), "tp", scatter_dimension=1, tiled=True
    ).astype(jnp.float32)
    attended = (residual.astype(jnp.float32) + attention_part).astype(jnp.bfloat16)
    stream = attended.astype(jnp.float32)
    squares = lax.psum(jnp.sum(stream * stream, axis=1), "tp")
    model_width = out_weight.shape[1]
    normed = (
        stream * lax.rsqrt(squares / model_width + EPSILON)[:, None] * norm_gain.astype(jnp.float32)
    ).astype(jnp.bfloat16)
    return exchange_slots(
        stream, normed, attended, routes, route_weight, gate_weight, up_weight, down_weight
    )


def exchange_slots(
    stream, normed, attended, routes, route_weight, gate_weight, up_weight, down_weight
):
    tokens = routes.shape[0]
    experts = lax.axis_size("req")
    top = routes.shape[1]
    capacity = max(2, tokens * top * 4 // (3 * experts))
    flat = routes.reshape(-1)
    onehot = (flat[:, None] == jnp.arange(experts, dtype=jnp.int32)[None, :]).astype(jnp.int32)
    slot = jnp.sum(jnp.cumsum(onehot, axis=0) * onehot, axis=1) - 1
    dest = (flat * capacity + slot).reshape(tokens, top)
    places = jnp.arange(experts * capacity, dtype=jnp.int32)
    chooser = jnp.any(dest[None, :, :] == places[:, None, None], axis=2).astype(jnp.bfloat16)
    whole = lax.all_gather(normed, "tp", axis=1, tiled=True)
    buffer = (
        jnp.dot(chooser, whole, preferred_element_type=jnp.float32)
        .astype(jnp.bfloat16)
        .reshape(experts, capacity, -1)
    )
    received = lax.all_to_all(buffer, "req", split_axis=0, concat_axis=0, tiled=True)
    gate = jnp.einsum("snd,df->snf", received, gate_weight[0], preferred_element_type=jnp.float32)
    up = jnp.einsum("snd,df->snf", received, up_weight[0], preferred_element_type=jnp.float32)
    hidden = (jax.nn.silu(gate) * up).astype(jnp.bfloat16)
    part_out = jnp.einsum(
        "snf,fd->snd", hidden, down_weight[0], preferred_element_type=jnp.float32
    ).astype(jnp.bfloat16)
    returned = lax.all_to_all(part_out, "req", split_axis=0, concat_axis=0, tiled=True)
    flat_out = returned.reshape(experts * capacity, -1)
    combined = jnp.zeros((tokens, flat_out.shape[1]), jnp.float32)
    for choice_index in range(top):
        picked = jnp.take(flat_out, dest[:, choice_index], axis=0).astype(jnp.float32)
        combined = combined + route_weight[:, choice_index : choice_index + 1] * picked
    expert_part = lax.psum_scatter(
        combined.astype(jnp.bfloat16), "tp", scatter_dimension=1, tiled=True
    ).astype(jnp.float32)
    mixed = (stream + expert_part).astype(jnp.bfloat16)
    return (attended, mixed)


MESH = pl.DeviceIdType.MESH


def coordinates():
    me = lax.axis_index("req")
    return me // 4, (me // 2) % 2, me % 2, lax.axis_index("tp")


def place(z, x, core, y):
    return {"req": (z * 2 + x) * 2 + core, "tp": y}


def prompt_kernel(block_ref, share_ref, keys_ref, mine_ref, send, recv, send_w, recv_w, local):
    me = lax.axis_index("req")
    y = lax.axis_index("tp")
    barrier = pltpu.get_barrier_semaphore()
    for step in range(1, 16):
        pl.semaphore_signal(
            barrier, inc=1, device_id={"req": (me + step) % 16, "tp": y}, device_id_type=MESH
        )
    pl.semaphore_wait(barrier, 15)
    rows = pl.ds(pl.multiple_of(me * 16, 16), 16)

    def shares(step):
        peer = (me + step) % 16
        return pltpu.make_async_remote_copy(
            share_ref.at[peer], mine_ref.at[me], send_w.at[step], recv_w.at[step],
            device_id={"req": peer, "tp": y}, device_id_type=MESH,
        )

    core, other = me % 2, me + 1 - 2 * (me % 2)

    def relay(step):
        source = (me + 2 * step) % 16
        lines = pl.ds(pl.multiple_of(source * 16, 16), 16)
        arrival = pltpu.make_async_remote_copy(
            keys_ref.at[:, lines, :], keys_ref.at[:, lines, :], send.at[8 - step],
            recv.at[8 - step], device_id={"req": source, "tp": y}, device_id_type=MESH,
        )
        passing = pltpu.make_async_remote_copy(
            keys_ref.at[:, lines, :], keys_ref.at[:, lines, :], send.at[8 + source // 2],
            recv.at[8 + source // 2], device_id={"req": other, "tp": y}, device_id_type=MESH,
        )
        return arrival, passing

    def arriving(step):
        source = (me + 2 * step) % 16 + 1 - 2 * core
        lines = pl.ds(pl.multiple_of(source * 16, 16), 16)
        return pltpu.make_async_remote_copy(
            keys_ref.at[:, lines, :], keys_ref.at[:, lines, :], send.at[8 + source // 2],
            recv.at[8 + source // 2], device_id={"req": other, "tp": y}, device_id_type=MESH,
        )

    def direct(step):
        return pltpu.make_async_remote_copy(
            block_ref, keys_ref.at[:, rows, :], send.at[step], recv.at[step],
            device_id={"req": (me + 2 * step) % 16, "tp": y}, device_id_type=MESH,
        )

    home = pltpu.make_async_remote_copy(
        block_ref, keys_ref.at[:, rows, :], send.at[8 + me // 2], recv.at[8 + me // 2],
        device_id={"req": other, "tp": y}, device_id_type=MESH,
    )
    for step in range(1, 8):
        direct(step).start()
    home.start()
    for step in range(1, 16):
        shares(step).start()
    own = pltpu.make_async_copy(block_ref, keys_ref.at[:, rows, :], local.at[0])
    own_share = pltpu.make_async_copy(share_ref.at[me], mine_ref.at[me], local.at[1])
    own.start()
    own_share.start()
    own.wait()
    own_share.wait()
    for step in range(1, 8):
        arrival, passing = relay(step)
        arrival.wait_recv()
        passing.start()
    for step in range(8):
        arriving(step).wait_recv()
    home.wait_send()
    for step in range(1, 8):
        direct(step).wait_send()
        relay(step)[1].wait_send()
    for step in range(1, 16):
        shares(step).wait()


def share_prompts(prompt_cache, share):
    groups, rows, width = prompt_cache.shape
    tokens = share.shape[2]
    return pl.pallas_call(
        prompt_kernel,
        out_shape=(
            jax.ShapeDtypeStruct((groups, rows * 16, width), prompt_cache.dtype),
            jax.ShapeDtypeStruct((16, 1, tokens), jnp.float32),
        ),
        in_specs=[pl.BlockSpec(memory_space=pltpu.VMEM)] * 2,
        out_specs=(pl.BlockSpec(memory_space=pltpu.VMEM),) * 2,
        scratch_shapes=[pltpu.SemaphoreType.DMA((16,))] * 4 + [pltpu.SemaphoreType.DMA((2,))],
        compiler_params=pltpu.CompilerParams(collective_id=0, has_side_effects=True),
    )(prompt_cache, share)


def greet():
    z, x, core, y = coordinates()
    barrier = pltpu.get_barrier_semaphore()
    for peer in (place(z, 1 - x, core, y), place(z, x, core, 1 - y), place(z, x, 1 - core, y)):
        pl.semaphore_signal(barrier, inc=1, device_id=peer, device_id_type=MESH)

    @pl.when(z < 3)
    def _():
        pl.semaphore_signal(barrier, inc=1, device_id=place(z + 1, x, core, y), device_id_type=MESH)

    @pl.when(z > 0)
    def _():
        pl.semaphore_signal(barrier, inc=1, device_id=place(z - 1, x, core, y), device_id_type=MESH)

    pl.semaphore_wait(barrier, 3 + (1 - z // 3) + (z + 2) // 3)


def spread_tokens(whole, send, recv):
    z, x, core, y = coordinates()
    half_rows, half_cols = whole.shape[1] // 2, whole.shape[2] // 2

    def piece(zp, xp, yp, half, cp):
        return whole.at[
            (zp * 2 + xp) * 2 + cp,
            pl.ds(half * half_rows, half_rows),
            pl.ds(pl.multiple_of(yp * half_cols, half_cols), half_cols),
        ]

    def hop(zp, xp, yp, half, cp, kind, peer):
        slot = zp * 8 + xp * 4 + yp * 2 + half
        part = piece(zp, xp, yp, half, cp)
        return pltpu.make_async_remote_copy(
            part, part, send.at[kind, slot], recv.at[cp, slot], device_id=peer, device_id_type=MESH
        )

    up, down = place(z + 1, x, core, y), place(z - 1, x, core, y)
    over_x, over_y, other = place(z, 1 - x, core, y), place(z, x, core, 1 - y), place(z, x, 1 - core, y)

    def column(zp, finish):
        for half in range(2):
            for go, kind, peer in (
                ((zp <= z) & (z < 3), 0, up), ((zp >= z) & (z > 0), 1, down)
            ):
                @pl.when(go)
                def _(kind=kind, peer=peer):
                    copy = hop(zp, x, y, half, core, kind, peer)
                    copy.wait_send() if finish else copy.start()
        for kind, peer, half in ((2, over_x, 0), (3, over_y, 1), (2, over_x, 1), (3, over_y, 0)):
            copy = hop(zp, x, y, half, core, kind, peer)
            copy.wait_send() if finish else copy.start()
        for half in range(2):
            copy = hop(zp, x, y, half, core, 4, other)
            copy.wait_send() if finish else copy.start()

    def beside(zp, finish):
        if not finish:
            for half in range(2):
                hop(zp, 1 - x, y, half, core, 2, over_x).wait_recv()
                hop(zp, x, 1 - y, half, core, 3, over_y).wait_recv()
        copies = [hop(zp, 1 - x, y, 0, core, 3, over_y), hop(zp, x, 1 - y, 1, core, 2, over_x)]
        for half in range(2):
            copies.append(hop(zp, 1 - x, y, half, core, 4, other))
            copies.append(hop(zp, x, 1 - y, half, core, 4, other))
        for copy in copies:
            copy.wait_send() if finish else copy.start()

    def diagonal(zp, finish):
        for half in range(2):
            copy = hop(zp, 1 - x, 1 - y, half, core, 4, other)
            if finish:
                copy.wait_send()
            else:
                hop(zp, 1 - x, 1 - y, half, core, 2, over_x).wait_recv()
                copy.start()

    def each(distance, work):
        if distance == 0:
            work(z)
            return

        @pl.when(z + distance < 4)
        def _():
            work(z + distance)

        @pl.when(z - distance >= 0)
        def _():
            work(z - distance)

    def arrive(zp):
        for half in range(2):
            hop(zp, x, y, half, core, 0, over_x).wait_recv()
        column(zp, False)

    column(z, False)
    for distance in range(1, 4):
        each(distance, arrive)
        each(distance - 1, lambda zp: beside(zp, False))
        if distance > 1:
            each(distance - 2, lambda zp: diagonal(zp, False))
    each(3, lambda zp: beside(zp, False))
    each(2, lambda zp: diagonal(zp, False))
    each(3, lambda zp: diagonal(zp, False))

    def close(zp, carry):
        for xp in range(2):
            for yp in range(2):
                for half in range(2):
                    hop(zp, xp, yp, half, 1 - core, 4, other).wait_recv()
        column(zp, True)
        beside(zp, True)
        diagonal(zp, True)
        return carry

    lax.fori_loop(0, 4, close, 0)


def return_sums(compute, acc, core_in, x_diag, y_diag, x_in, y_in, up_in, down_in, sems):
    z, x, core, y = coordinates()
    rows, half_cols = acc.shape[2], acc.shape[3] // 2
    half_rows = rows // 2
    up, down = place(z + 1, x, core, y), place(z - 1, x, core, y)
    over_x, over_y, other = place(z, 1 - x, core, y), place(z, x, core, 1 - y), place(z, x, 1 - core, y)
    mine = pl.ds(pl.multiple_of(y * half_cols, half_cols), half_cols)
    theirs = pl.ds(pl.multiple_of((1 - y) * half_cols, half_cols), half_cols)
    top, low = pl.ds(0, half_rows), pl.ds(half_rows, half_rows)

    def copy(source, target, kind, zp, peer):
        return pltpu.make_async_remote_copy(
            source, target, sems.at[0, kind, zp], sems.at[1, kind, zp],
            device_id=peer, device_id_type=MESH,
        )

    def block(zp, xp, cp):
        return acc.at[zp, xp * 2 + cp]

    def core_copy(zp, xp):
        return copy(block(zp, xp, 1 - core), core_in.at[zp, xp], xp, zp, other)

    def diag_copies(zp):
        far = block(zp, 1 - x, core)
        return (
            copy(far.at[top, theirs], y_diag.at[zp], 2, zp, over_y),
            copy(far.at[low, theirs], x_diag.at[zp], 3, zp, over_x),
        )

    def free_copies(zp):
        return (
            copy(block(zp, 1 - x, core).at[low, mine], x_in.at[zp, low], 4, zp, over_x),
            copy(block(zp, x, core).at[top, theirs], y_in.at[zp, top], 5, zp, over_y),
        )

    def last_copies(zp):
        return (
            copy(block(zp, 1 - x, core).at[top, mine], x_in.at[zp, top], 6, zp, over_x),
            copy(block(zp, x, core).at[low, theirs], y_in.at[zp, low], 7, zp, over_y),
        )

    def up_copy(zp):
        return copy(block(zp, x, core).at[:, mine], up_in.at[zp], 8, zp, up)

    def down_copy(zp):
        return copy(block(zp, x, core).at[:, mine], down_in.at[zp], 9, zp, down)

    def add(target, *terms):
        total = target[...].astype(jnp.float32)
        for term in terms:
            total = total + term[...].astype(jnp.float32)
        target[...] = total.astype(target.dtype)

    def cores(zp):
        for xp in range(2):
            core_copy(zp, xp).wait_recv()
            add(block(zp, xp, core), core_in.at[zp, xp])
        for item in diag_copies(zp) + free_copies(zp):
            item.start()

    def corners(zp):
        from_y, from_x = diag_copies(zp)
        over_x_copy, over_y_copy = last_copies(zp)
        from_y.wait_recv()
        add(block(zp, 1 - x, core).at[top, mine], y_diag.at[zp])
        over_x_copy.start()
        from_x.wait_recv()
        add(block(zp, x, core).at[low, theirs], x_diag.at[zp])
        over_y_copy.start()

    def columns(zp):
        for item in free_copies(zp) + last_copies(zp):
            item.wait_recv()
        own = block(zp, x, core).at[:, mine]
        add(own, x_in.at[zp], y_in.at[zp])

        @pl.when((z > 0) & (zp >= z))
        def _():
            up_copy(zp).wait_recv()
            add(own, up_in.at[zp])

        @pl.when((z < 3) & (zp <= z))
        def _():
            down_copy(zp).wait_recv()
            add(own, down_in.at[zp])

        @pl.when(zp > z)
        def _():
            up_copy(zp).start()

        @pl.when(zp < z)
        def _():
            down_copy(zp).start()

    def turn(step):
        return (3 - step // 2) * (1 - step % 2) + (step // 2) * (step % 2)

    def stage(step, carry):
        @pl.when(step < 4)
        def _():
            zp = turn(step)
            compute(zp)
            for xp in range(2):
                core_copy(zp, xp).start()

        @pl.when((step >= 1) & (step < 5))
        def _():
            cores(turn(step - 1))

        @pl.when((step >= 2) & (step < 6))
        def _():
            corners(turn(step - 2))

        @pl.when(step >= 3)
        def _():
            columns(turn(step - 3))

        return carry

    lax.fori_loop(0, 7, stage, 0)

    def close(zp, carry):
        for xp in range(2):
            core_copy(zp, xp).wait_send()
        for item in diag_copies(zp) + free_copies(zp) + last_copies(zp):
            item.wait_send()

        @pl.when(zp > z)
        def _():
            up_copy(zp).wait_send()

        @pl.when(zp < z)
        def _():
            down_copy(zp).wait_send()

        return carry

    lax.fori_loop(0, 4, close, 0)
    return block(z, x, core).at[:, mine]


def expert_kernel(
    projected, residual, gain, chooser, slot_weight, gate_hbm, up_hbm, down_hbm,
    attended, mixed,
    whole, outgoing, incoming, squares_out, squares_in, gate_w, up_w, down_w, rows, hidden,
    acc, core_in, x_diag, y_diag, x_in, y_in, up_in, down_in,
    pair_sems, load_sems, send, recv, sems,
):
    z, x, core, y = coordinates()
    half_cols = residual.shape[1]
    loads = [
        pltpu.make_async_copy(source, target, load_sems.at[index])
        for index, (source, target) in enumerate(
            ((gate_hbm, gate_w), (up_hbm, up_w), (down_hbm, down_w))
        )
    ]
    for load in loads:
        load.start()
    mine = pl.ds(pl.multiple_of(y * half_cols, half_cols), half_cols)
    theirs = pl.ds(pl.multiple_of((1 - y) * half_cols, half_cols), half_cols)
    over_y = place(z, x, core, 1 - y)
    outgoing[...] = projected[:, theirs].astype(jnp.bfloat16)
    greet()
    swap = pltpu.make_async_remote_copy(
        outgoing, incoming, pair_sems.at[0], pair_sems.at[1], device_id=over_y, device_id_type=MESH
    )
    swap.start()
    swap.wait()
    stream = residual[...].astype(jnp.float32) + projected[:, mine] + incoming[...].astype(jnp.float32)
    attended[...] = stream.astype(jnp.bfloat16)
    stream = attended[...].astype(jnp.float32)
    sums = jnp.sum(stream * stream, axis=1, keepdims=True)
    squares_out[...] = jnp.broadcast_to(sums, squares_out.shape)
    pair = pltpu.make_async_remote_copy(
        squares_out, squares_in, pair_sems.at[2], pair_sems.at[3],
        device_id=over_y, device_id_type=MESH,
    )
    pair.start()
    pair.wait()
    both = sums + squares_in[:, :1]
    scaled = stream * lax.rsqrt(both / (2 * half_cols) + EPSILON) * gain[...].astype(jnp.float32)
    whole[(z * 2 + x) * 2 + core, :, mine] = scaled.astype(jnp.bfloat16)
    spread_tokens(whole, send, recv)
    for load in loads:
        load.wait()
    capacity = chooser.shape[1]

    def compute(zp):
        for index in range(4):
            picked = jnp.dot(
                chooser[zp * 4 + index], whole[zp * 4 + index], preferred_element_type=jnp.float32
            )
            rows[pl.ds(index * capacity, capacity), :] = picked.astype(jnp.bfloat16)
        across = (((1,), (1,)), ((), ()))
        gate = lax.dot_general(rows[...], gate_w[...], across, preferred_element_type=jnp.float32)
        up = lax.dot_general(rows[...], up_w[...], across, preferred_element_type=jnp.float32)
        level = slot_weight[pl.ds(pl.multiple_of(zp * 4 * capacity, 4 * capacity), 4 * capacity), :]
        hidden[...] = (gate / (1.0 + jnp.exp(-gate)) * up * level).astype(jnp.bfloat16)
        part = jnp.dot(hidden[...], down_w[...], preferred_element_type=jnp.float32)
        part = part.astype(jnp.bfloat16)
        for index in range(4):
            acc[zp, index] = lax.dot_general(
                chooser[zp * 4 + index], part[index * capacity : (index + 1) * capacity],
                (((0,), (0,)), ((), ())), preferred_element_type=jnp.float32,
            ).astype(jnp.bfloat16)

    own = return_sums(compute, acc, core_in, x_diag, y_diag, x_in, y_in, up_in, down_in, sems)
    mixed[...] = (attended[...].astype(jnp.float32) + own[...].astype(jnp.float32)).astype(jnp.bfloat16)


def run_experts(projected, residual, gain, chooser, slot_weight, gate_w, up_w, down_w):
    tokens, width = projected.shape
    half = residual.shape[1]
    capacity = chooser.shape[1]
    units = gate_w.shape[0]
    bf16, f32 = jnp.bfloat16, jnp.float32
    dma = pltpu.SemaphoreType.DMA
    vmem = pl.BlockSpec(memory_space=pltpu.VMEM)
    anywhere = pl.BlockSpec(memory_space=pl.ANY)
    return pl.pallas_call(
        expert_kernel,
        out_shape=(jax.ShapeDtypeStruct((tokens, half), bf16),) * 2,
        in_specs=[vmem] * 5 + [anywhere] * 3,
        out_specs=(vmem, vmem),
        scratch_shapes=[
            pltpu.VMEM((16, tokens, width), bf16),
            pltpu.VMEM((tokens, half), bf16),
            pltpu.VMEM((tokens, half), bf16),
            pltpu.VMEM((tokens, 128), f32),
            pltpu.VMEM((tokens, 128), f32),
            pltpu.VMEM((units, width), bf16),
            pltpu.VMEM((units, width), bf16),
            pltpu.VMEM((units, width), bf16),
            pltpu.VMEM((4 * capacity, width), bf16),
            pltpu.VMEM((4 * capacity, units), bf16),
            pltpu.VMEM((4, 4, tokens, width), bf16),
            pltpu.VMEM((4, 2, tokens, width), bf16),
            pltpu.VMEM((4, tokens // 2, half), bf16),
            pltpu.VMEM((4, tokens // 2, half), bf16),
            pltpu.VMEM((4, tokens, half), bf16),
            pltpu.VMEM((4, tokens, half), bf16),
            pltpu.VMEM((4, tokens, half), bf16),
            pltpu.VMEM((4, tokens, half), bf16),
            dma((4,)),
            dma((3,)),
            dma((5, 32)),
            dma((2, 32)),
            dma((2, 10, 4)),
        ],
        compiler_params=pltpu.CompilerParams(
            collective_id=1, has_side_effects=True, vmem_limit_bytes=58 << 20
        ),
    )(projected, residual, gain, chooser, slot_weight, gate_w, up_w, down_w)


def on_block(
    queries, stretch_cache, prefix_pool, page_table, prefix_len, prompt_cache, prompt_len,
    group_ids, absorb_weight, value_weight, out_weight, residual, norm_gain, routes,
    route_weight, gate_weight, up_weight, down_weight,
):
    tokens, heads, width = queries.shape
    nope, rank = absorb_weight.shape[1], value_weight.shape[1]
    experts, top = lax.axis_size("req"), routes.shape[1]
    capacity = max(2, tokens * top * 4 // (3 * experts))
    me = lax.axis_index("req")
    choice = routes[:, :, None] == jnp.arange(experts, dtype=jnp.int32)[None, None, :]
    share = jnp.sum(jnp.where(choice, route_weight[:, :, None], 0.0), axis=1)
    prompts, mine = share_prompts(prompt_cache, share.T[:, None, :])
    mine = mine[:, 0, :]
    named = mine > 0.0
    before = jnp.arange(tokens)[:, None] <= jnp.arange(tokens)[None, :]
    slot = jnp.dot(
        named.astype(jnp.bfloat16), before.astype(jnp.bfloat16), preferred_element_type=jnp.float32
    ).astype(jnp.int32) - 1
    picks = (
        slot[:, None, :] == jnp.arange(capacity, dtype=jnp.int32)[None, :, None]
    ) & named[:, None, :]
    chooser = picks.astype(jnp.bfloat16)
    slot_weight = jnp.sum(jnp.where(picks, mine[:, None, :], 0.0), axis=2).reshape(-1, 1)

    requests = jnp.arange(group_ids.shape[0], dtype=jnp.int32) == me
    group = jnp.sum(jnp.where(requests, group_ids, 0))
    own_length = jnp.sum(jnp.where(requests, prefix_len, 0))
    prompt_length = jnp.where(group == 0, prompt_len[0], prompt_len[1])
    pages, page = prefix_pool.shape[:2]
    order = jnp.arange(pages, dtype=jnp.int32)
    logical = jnp.sum(
        jnp.where(page_table[0][None, :] == order[:, None], order[None, :], 0), axis=1
    )
    prefix_at = (logical[:, None] * page + jnp.arange(page, dtype=jnp.int32)[None, :]).reshape(-1)
    prompt = jnp.where(group == 0, prompts[0], prompts[1])
    keys = jnp.concatenate(
        [stretch_cache, prompt, prefix_pool.reshape(pages * page, -1)], axis=0
    )
    seen = jnp.concatenate(
        [jnp.arange(prompt.shape[0]) < prompt_length, prefix_at < own_length]
    )
    token = jnp.arange(tokens)
    visible = jnp.concatenate(
        [
            token[None, :] <= token[:, None],
            jnp.broadcast_to(seen[None, :], (tokens, seen.shape[0])),
        ],
        axis=1,
    )
    turned = jnp.transpose(queries, (1, 0, 2))
    absorbed = jnp.concatenate(
        [
            jnp.einsum(
                "htn,hnr->htr", turned[:, :, :nope], absorb_weight,
                preferred_element_type=jnp.float32,
            ).astype(jnp.bfloat16),
            turned[:, :, nope:],
        ],
        axis=2,
    )
    scores = jnp.einsum("htc,kc->htk", absorbed, keys, preferred_element_type=jnp.float32)
    scores = jnp.where(visible[None], scores * width ** (-0.5), NEGATIVE)
    weights = jnp.exp(scores - jnp.max(scores, axis=2, keepdims=True))
    weights = jnp.where(visible[None], weights, 0.0)
    totals = jnp.sum(weights, axis=2, keepdims=True)
    latent = jnp.einsum(
        "htk,kr->htr", weights.astype(jnp.bfloat16), keys[:, :rank],
        preferred_element_type=jnp.float32,
    )
    latent = (latent / totals).astype(jnp.bfloat16)
    heads_out = jnp.einsum(
        "htr,hrv->thv", latent, value_weight, preferred_element_type=jnp.float32
    ).astype(jnp.bfloat16)
    projected = jnp.dot(
        heads_out.reshape(tokens, -1), out_weight, preferred_element_type=jnp.float32
    )
    return run_experts(
        projected, residual, norm_gain[None, :], chooser, slot_weight,
        jnp.swapaxes(gate_weight[0], 0, 1), jnp.swapaxes(up_weight[0], 0, 1), down_weight[0],
    )


def solution(mesh):
    in_specs = (
        P("req", "tp", None),
        P("req", None),
        P("req", None, None),
        P("req", None),
        P(),
        P(None, "req", None),
        P(),
        P(),
        P("tp", None, None),
        P("tp", None, None),
        P("tp", None),
        P("req", "tp"),
        P("tp"),
        P("req", None),
        P("req", None),
        P("req", None, "tp"),
        P("req", None, "tp"),
        P("req", "tp", None),
    )
    out_specs = (P("req", "tp"), P("req", "tp"))
    body = on_block if mesh.shape["req"] == 16 and mesh.shape["tp"] == 2 else on_device
    return jax.shard_map(
        body, mesh=mesh, in_specs=in_specs, out_specs=out_specs, check_vma=False
    )
```
